256 devices in a mesh: box: 64 (over x, y, z_lo), angle: 4 (over z_hi, core).
Axes of the slice: x: 4, y: 4, z: 8 (z_hi: 2, z_lo: 4; z = z_hi * 4 + z_lo), core: 2. Of those that a mesh axis runs over, the one named last changes fastest.
Arguments:
- coeffs: float32 [4, 2048, 16, 512], P('angle', 'box'), may hold values from -6 to 6
- src_pos: int32 [4, 64, 2], P('angle'), may hold values from 0 to 63
- tgt_pos: int32 [2048, 2], P('box'), may hold values from 0 to 63
- interp: float32 [2, 512, 512], replicated, may hold values from -0.25 to 0.25
Outputs:
- fields: float32 [2048, 16, 512], P('box')
The draws below stay inside these ranges and needn't reach their ends.
All inputs are finite; a program needn't handle non-finite values.
Results may differ from the reference program's by a relative error of at most 0.00016.
Values sent between devices are 32-bit elements; how exact they have to be, the bound alone decides.
A program may use at most 64 MiB of HBM per device.

```python
import math
import jax
import jax.numpy as jnp
from jax import lax

CHEB = 16
F = 16
P_SIZE = 32
ANGLES = 4
SLOTS = 2048
N_BOX = 64


def with_ends(entries, stream_key, least, high):
    longest = entries.shape.index(max(entries.shape))
    spots = []
    for shift in (0, 1):
        where = [jax.random.randint(jax.random.fold_in(stream_key, axis), (), 0, length) for axis, length in enumerate(entries.shape)]
        where[longest] = (where[longest] + shift) % entries.shape[longest]
        spots.append(tuple(where))
    return entries.at[spots[0]].set(least).at[spots[1]].set(high)


def block_levels(stream_key, shape, shards, smallest, high):
    gain, own = 1.0, jax.random.fold_in(stream_key, 6)
    for dim, parts in shards:
        heights = jnp.exp(jax.random.uniform(jax.random.fold_in(own, dim), (parts,), jnp.float32, smallest / len(shards), high / len(shards)))
        gain = gain * jnp.repeat(heights, shape[dim] // parts).reshape([-1 if axis == dim else 1 for axis in range(len(shape))])
    return gain


def scatter_about(stream_key, dims, scale, limit, cuts=(), held_as=jnp.bfloat16):
    loudness = block_levels(stream_key, dims, cuts, -0.22, 0.18) if cuts else 1.0
    array = jax.random.normal(stream_key, dims, jnp.float32) * scale * loudness
    return jnp.minimum(jnp.maximum(array, -limit), limit).astype(held_as)


def setup_inputs(seed: int = 0) -> dict:
    seeds = jax.random.split(jax.random.key(seed), 5)
    return {
        "coeffs": scatter_about(seeds[0], (ANGLES, SLOTS, F, 2 * CHEB * CHEB), 1.0, 6.0, ((0, 4), (1, 64)), jnp.float32),
        "src_pos": with_ends(jax.random.randint(seeds[1], (ANGLES, N_BOX, 2), 0, 64), jax.random.fold_in(seeds[1], 1), 0, 63).astype(jnp.int32),
        "tgt_pos": with_ends(jax.random.randint(seeds[2], (SLOTS, 2), 0, 64), jax.random.fold_in(seeds[2], 1), 0, 63).astype(jnp.int32),
        "interp": scatter_about(seeds[3], (2, 2 * CHEB * CHEB, 2 * CHEB * CHEB), (2 * CHEB * CHEB) ** -0.5, 0.25, (), jnp.float32),
    }


PHASE_SCALE = math.pi / 16.0


def cheb_nodes(node_count):
    tick_values = jnp.arange(node_count, dtype=jnp.float32)
    return jnp.cos(math.pi * (2.0 * tick_values + 1.0) / (2.0 * node_count))


def node_grid(node_count):
    node_line = cheb_nodes(node_count)
    return jnp.repeat(node_line, node_count), jnp.tile(node_line, node_count)


def rotate(values, phase_angle):
    points = values.shape[-1] // 2
    real_part = values[..., :points]
    imag_part = values[..., points:]
    cosine = jnp.cos(phase_angle)
    sine_part = jnp.sin(phase_angle)
    return jnp.concatenate([real_part * cosine - imag_part * sine_part, real_part * sine_part + imag_part * cosine], axis=-1)


def plane_phase(coord_pair, factor, node_first, node_second):
    return factor * (coord_pair[..., 0:1].astype(jnp.float32) * node_first + coord_pair[..., 1:2].astype(jnp.float32) * node_second)


def lane_pass(state, coords, targets, interp, node_first, node_second):
    device_ids = jnp.arange(N_BOX, dtype=jnp.int32)
    half_slots = P_SIZE // 2
    points = CHEB * CHEB
    for height in range(int(N_BOX).bit_length() - 1):
        stride = 2 ** height
        bit_values = (device_ids // stride) % 2
        low_ids = device_ids - bit_values * stride
        high_ids = low_ids + stride
        halves = state.reshape(N_BOX, 2, half_slots, F, 2 * points)
        spread = -PHASE_SCALE / (2.0 ** height)
        child_zero = rotate(halves[low_ids, bit_values], plane_phase(coords[low_ids], spread, node_first, node_second)[:, None, None, :])
        child_one = rotate(halves[high_ids, bit_values], plane_phase(coords[high_ids], spread, node_first, node_second)[:, None, None, :])
        rows = jnp.concatenate([child_zero.reshape(-1, points), child_one.reshape(-1, points)], axis=1)
        mixed = jnp.dot(rows, interp[height % 2], precision=lax.Precision.HIGHEST, preferred_element_type=jnp.float32)
        target_zero = mixed[:, :points].reshape(N_BOX, half_slots, F, 2 * points)
        target_one = mixed[:, points:].reshape(N_BOX, half_slots, F, 2 * points)
        state = jnp.concatenate([target_zero, target_one], axis=1)
        outer = plane_phase(targets, PHASE_SCALE / (height + 1.0), node_first, node_second)
        state = rotate(state, outer[:, :, None, :])
        coords = coords[low_ids] + coords[high_ids]
    return state


def reference(coeffs, src_pos, tgt_pos, interp):
    node_first, node_second = node_grid(CHEB)
    targets = tgt_pos.reshape(N_BOX, P_SIZE, 2)

    def add_lane(running, lane_items):
        lane_coeffs, lane_coords = lane_items
        state = lane_coeffs.reshape(N_BOX, P_SIZE, F, 2 * CHEB * CHEB)
        return running + lane_pass(state, lane_coords, targets, interp, node_first, node_second), None

    running = jnp.zeros((N_BOX, P_SIZE, F, 2 * CHEB * CHEB), jnp.float32)
    summed, unused = lax.scan(add_lane, running, (coeffs, src_pos))
    return summed.reshape(N_BOX * P_SIZE, F, 2 * CHEB * CHEB)
```

```python
import math

import jax
import jax.numpy as jnp
from jax import lax
from jax.experimental import pallas as pl
from jax.experimental.pallas import tpu as pltpu
from jax.sharding import PartitionSpec as P

MESH = pl.DeviceIdType.MESH
F32 = jnp.float32
BF16 = jnp.bfloat16
TWO_PI = 2.0 * math.pi


def cos_sin(turns):
    quarter = jnp.floor(turns * 4.0 + 0.5)
    x = (turns - quarter * 0.25) * TWO_PI
    x2 = x * x
    s = x * (1.0 + x2 * (-1.0 / 6 + x2 * (1.0 / 120 + x2 * (-1.0 / 5040 + x2 * (1.0 / 362880)))))
    c = 1.0 + x2 * (-0.5 + x2 * (1.0 / 24 + x2 * (-1.0 / 720 + x2 * (1.0 / 40320))))
    qi = quarter.astype(jnp.int32)
    odd = (qi & 1) == 1
    s, c = jnp.where(odd, c, s), jnp.where(odd, s, c)
    s = jnp.where((qi & 2) == 2, -s, s)
    c = jnp.where(((qi + 1) & 2) == 2, -c, c)
    return c, s


def split(value):
    hi = value.astype(BF16)
    lo = (value - hi.astype(F32)).astype(BF16)
    return hi, lo


def kernel(
    x_ref, aux_ref, w_ref, o_ref,
    aux_a, aux_b, auxf, ra, wf, whi, wlo, lhi, llo, out, tab1, tab2, tab5, bsend, brecv, csend, crecv, dsend,
    sa_s, sa_r, sx_s, sx_r, ba_s, ba_r, bx_s, bx_r, c_s, c_r, d_s, d_r, e_s, e_r, loc,
):
    box = lax.axis_index("box")
    ang = lax.axis_index("angle")
    xy = box // 4
    zlo = box % 4
    n = ang * 4 + zlo
    core = ang % 2
    z8 = (ang // 2) * 4 + zlo

    def zdev(m):
        return {"box": xy * 4 + m % 4, "angle": m // 4}

    def xydev(m):
        return {"box": m * 4 + zlo, "angle": ang}

    def z8dev(m):
        return {"box": xy * 4 + m % 4, "angle": (m // 4) * 2 + core}

    sib = {"box": box, "angle": ang + 1 - 2 * core}

    def each(lo, hi, fn):
        def step(k, carry):
            fn(k)
            return carry

        lax.fori_loop(lo, hi, step, 0)

    def remote(src, dst, ss, rs, dev):
        return pltpu.make_async_remote_copy(src, dst, ss, rs, device_id=dev, device_id_type=MESH)

    wcopy = pltpu.make_async_copy(w_ref, wf, loc.at[0])
    wcopy.start()
    own_x = pltpu.make_async_copy(x_ref.at[:, n], ra.at[n], loc.at[1])
    own_x.start()
    own_aux = pltpu.make_async_copy(aux_ref, aux_a.at[n], loc.at[2])
    own_aux.start()

    barrier = pltpu.get_barrier_semaphore()
    each(1, 16, lambda k: pl.semaphore_signal(barrier, inc=1, device_id=zdev((n + k) % 16), device_id_type=MESH))
    each(1, 16, lambda k: pl.semaphore_signal(barrier, inc=1, device_id=xydev((xy + k) % 16), device_id_type=MESH))
    pl.semaphore_wait(barrier, 30)

    def send_aux_a(k):
        return remote(aux_ref, aux_a.at[n], sa_s.at[k], sa_r.at[k], zdev((n + k) % 16))

    def send_a(k):
        m = (n + k) % 16
        return remote(x_ref.at[:, m], ra.at[n], sx_s.at[k], sx_r.at[k], zdev(m))

    each(1, 16, lambda k: send_aux_a(k).start())
    each(1, 16, lambda k: send_a(k).start())

    own_aux.wait()
    each(1, 16, lambda k: send_aux_a(k).wait())
    auxf[...] = jnp.concatenate([aux_a[i, 0:1, :] for i in range(16)], axis=0)
    own_auxb = pltpu.make_async_copy(auxf, aux_b.at[xy], loc.at[3])
    own_auxb.start()

    def send_aux_b(k):
        return remote(auxf, aux_b.at[xy], ba_s.at[k], ba_r.at[k], xydev((xy + k) % 16))

    each(1, 16, lambda k: send_aux_b(k).start())

    wcopy.wait()
    for level in range(2):
        for t in range(2):
            hi, lo = split(wf[level, :, t * 256 : (t + 1) * 256])
            whi[level, t] = hi
            wlo[level, t] = lo

    point = lax.broadcasted_iota(jnp.int32, (8, 256), 1)
    node_u, _ = cos_sin((2.0 * (point // 16).astype(F32) + 1.0) / 64.0)
    node_v, _ = cos_sin((2.0 * (point % 16).astype(F32) + 1.0) / 64.0)
    lane = lax.broadcasted_iota(jnp.int32, (16, 128), 1)

    def tgt(a, t):
        base = 2 * (t * 16 + n)
        tx = jnp.sum(jnp.where(lane == base, a, 0.0), axis=1, keepdims=True)
        ty = jnp.sum(jnp.where(lane == base + 1, a, 0.0), axis=1, keepdims=True)
        return tx, ty

    def src(a, b):
        return a[:, 64 + 2 * b : 65 + 2 * b], a[:, 65 + 2 * b : 66 + 2 * b]

    def phases(cu, cv):
        rows = cu.shape[0]
        cu = jnp.broadcast_to(cu, (rows, 256))
        cv = jnp.broadcast_to(cv, (rows, 256))
        u = jnp.concatenate([node_u] * (rows // 8), axis=0)
        v = jnp.concatenate([node_v] * (rows // 8), axis=0)
        return cos_sin(cu * u + cv * v)

    def ts(level):
        return 1.0 / (32.0 * (level + 1.0))

    def cs(level):
        return -1.0 / (32.0 * 2.0**level)

    a0 = auxf[...]
    s0 = src(a0, 0)
    c, s = phases(s0[0] * cs(0), s0[1] * cs(0))
    tab1[0, 0], tab1[0, 1] = c, s
    for t in range(2):
        tx, ty = tgt(a0, t)
        for level in range(2):
            cx, cy = src(a0, level + 1)
            c, s = phases(tx * ts(level) + cx * cs(level + 1), ty * ts(level) + cy * cs(level + 1))
            tab1[1 + 2 * level + t, 0], tab1[1 + 2 * level + t, 1] = c, s

    own_auxb.wait()
    each(1, 16, lambda k: send_aux_b(k).wait())

    def table2(i):
        d, t = i // 2, i % 2
        a = aux_b[d]
        tx, ty = tgt(a, t)
        for level in (2, 3, 4):
            cx, cy = src(a, level + 1)
            c, s = phases(tx * ts(level) + cx * cs(level + 1), ty * ts(level) + cy * cs(level + 1))
            tab2[level - 2, i, 0], tab2[level - 2, i, 1] = c, s

    each(0, 32, table2)
    low = lax.broadcasted_iota(jnp.int32, (8, 128), 0) < 4
    low2 = lax.broadcasted_iota(jnp.int32, (8, 256), 0) < 4

    def table5(i):
        jp, t = i // 2, i % 2
        a = jnp.where(low, aux_b[jp, 0:8, :], aux_b[jp + 8, 0:8, :])
        base = 2 * (t * 16 + n)
        lane8 = lax.broadcasted_iota(jnp.int32, (8, 128), 1)
        tx = jnp.sum(jnp.where(lane8 == base, a, 0.0), axis=1, keepdims=True)
        ty = jnp.sum(jnp.where(lane8 == base + 1, a, 0.0), axis=1, keepdims=True)
        c, s = phases(tx * ts(5), ty * ts(5))
        tab5[i, 0], tab5[i, 1] = c, s

    each(0, 16, table5)

    def rotated(re, im, c, s):
        return re * c - im * s, re * s + im * c

    def put(j, c, re, im):
        h, l = split(re)
        lhi[c, j, 0], llo[c, j, 0] = h, l
        h, l = split(im)
        lhi[c, j, 1], llo[c, j, 1] = h, l

    def place(d, t, bit):
        stride = 1 << bit
        c = (d // stride) % 2
        return d - c * stride + t * stride, c

    def matmul(level, rows, block):
        w = level % 2

        def step(i):
            sl = pl.ds(i * (block // 32), block // 32)
            for t in range(2):
                acc = None
                for c in range(2):
                    h = lhi[c, sl].reshape(block, 256)
                    l = llo[c, sl].reshape(block, 256)
                    wh = whi[w, t, c * 256 : (c + 1) * 256, :]
                    wl = wlo[w, t, c * 256 : (c + 1) * 256, :]
                    for a, b in ((h, wh), (l, wh), (h, wl)):
                        p = jnp.dot(a, b, preferred_element_type=F32)
                        acc = p if acc is None else acc + p
                out[t, sl] = acc.reshape(block // 32, 2, 16, 256)

        each(0, rows // block, step)

    own_x.wait()
    each(1, 16, lambda k: send_a(k).wait())

    def build0(i):
        d, t = i // 2, i % 2
        v = ra[d, t]
        c = tab1[0, 0, pl.ds(d, 1), :]
        s = tab1[0, 1, pl.ds(d, 1), :]
        re, im = rotated(v[:, 0:256], v[:, 256:512], c, s)
        j, ch = place(d, t, 0)
        put(j, ch, re, im)

    each(0, 32, build0)
    matmul(0, 512, 128)

    def build1(i):
        d, t = i // 2, i % 2
        c = tab1[1 + t, 0, pl.ds(d, 1), :]
        s = tab1[1 + t, 1, pl.ds(d, 1), :]
        re, im = rotated(out[t, d, 0], out[t, d, 1], c, s)
        j, ch = place(d, t, 1)
        put(j, ch, re, im)

    each(0, 32, build1)
    matmul(1, 512, 128)

    def post1(i):
        d, t = i // 2, i % 2
        c = tab1[3 + t, 0, pl.ds(d, 1), :]
        s = tab1[3 + t, 1, pl.ds(d, 1), :]
        re, im = rotated(out[t, d, 0], out[t, d, 1], c, s)
        rows = pl.ds(d, 16, stride=16)
        bsend[t, 0, rows, :] = re[:, 0:128]
        bsend[t, 1, rows, :] = re[:, 128:256]
        bsend[t, 2, rows, :] = im[:, 0:128]
        bsend[t, 3, rows, :] = im[:, 128:256]

    each(0, 32, post1)

    def bchunk(f):
        return bsend.at[:, :, pl.ds(pl.multiple_of(f * 16, 16), 16), :]

    own_b = pltpu.make_async_copy(bchunk(xy), brecv.at[xy], loc.at[4])
    own_b.start()

    def send_b(k):
        m = (xy + k) % 16
        return remote(bchunk(m), brecv.at[xy], bx_s.at[k], bx_r.at[k], xydev(m))

    each(1, 16, lambda k: send_b(k).start())
    own_b.wait()
    each(1, 16, lambda k: send_b(k).wait())

    def build2(i):
        d, t = i // 2, i % 2
        j, ch = place(d, t, 0)
        re = jnp.concatenate([brecv[d, t, 0], brecv[d, t, 1]], axis=1)
        im = jnp.concatenate([brecv[d, t, 2], brecv[d, t, 3]], axis=1)
        put(j, ch, re, im)

    each(0, 32, build2)
    matmul(2, 512, 128)
    for bit in (1, 2):

        def build34(i):
            d, t = i // 2, i % 2
            re, im = rotated(out[t, d, 0], out[t, d, 1], tab2[bit - 1, i, 0], tab2[bit - 1, i, 1])
            j, ch = place(d, t, bit)
            put(j, ch, re, im)

        each(0, 32, build34)
        matmul(bit + 2, 512, 128)

    def build5(d):
        parts = []
        for t in range(2):
            i = 2 * d + t
            re, im = rotated(out[t, d, 0], out[t, d, 1], tab2[2, i, 0], tab2[2, i, 1])
            parts.append((re[0:8] + re[8:16], im[0:8] + im[8:16]))
        packed = []
        for p in range(2):
            v0, v1 = parts[0][p], parts[1][p]
            packed.append(jnp.where(low2, v0, v1) + pltpu.roll(jnp.where(low2, v1, v0), 4, 0))
        value = jnp.concatenate(packed, axis=0)
        h, l = split(value)
        jp, ch = d % 8, d // 8
        lhi[ch, jp // 2, jp % 2] = h
        llo[ch, jp // 2, jp % 2] = l

    each(0, 16, build5)
    matmul(5, 128, 128)

    def post5(jp):
        fin = []
        for t in range(2):
            v = out[t, jp // 2, jp % 2]
            i = 2 * jp + t
            fin.append(rotated(v[0:8], v[8:16], tab5[i, 0], tab5[i, 1]))
        for p in range(2):
            f0, f1 = fin[0][p], fin[1][p]
            g0 = jnp.where(low2, f0, pltpu.roll(f1, 4, 0))
            g1 = jnp.where(low2, pltpu.roll(f0, 4, 0), f1)
            for half in range(2):
                csend[jp, 2 * p + half] = g0[:, half * 128 : half * 128 + 128]
                csend[jp + 8, 2 * p + half] = g1[:, half * 128 : half * 128 + 128]

    each(0, 8, post5)

    def cslot():
        return crecv.at[:, pl.ds(pl.multiple_of(xy * 8, 8), 8), :]

    own_c = pltpu.make_async_copy(csend.at[xy], cslot(), loc.at[5])
    own_c.start()

    def send_c(k):
        m = (xy + k) % 16
        return remote(csend.at[m], cslot(), c_s.at[k], c_r.at[k], xydev(m))

    each(1, 16, lambda k: send_c(k).start())
    own_c.wait()
    each(1, 16, lambda k: send_c(k).wait())

    def turn(r):
        z, t = r % 4, r // 4
        for cb in range(4):
            dsend[z, t, :, cb * 128 : cb * 128 + 128] = crecv[cb, pl.ds(r, 16, stride=8), :]

    each(0, 8, turn)

    own_d = pltpu.make_async_copy(dsend.at[zlo], o_ref.at[:, n], loc.at[6])
    own_d.start()

    def send_d(k):
        m = (z8 + k) % 8
        return remote(dsend.at[m % 4], o_ref.at[:, n], d_s.at[k], d_r.at[k], z8dev(m))

    each(1, 8, lambda k: send_d(k).start())

    def qof(m):
        return ((m // 4) * 2 + core) * 4 + m % 4

    def send_e0():
        return remote(dsend.at[zlo], o_ref.at[:, n], e_s.at[0], e_r.at[0], sib)

    def send_e(k):
        q = qof((z8 + 8 - k) % 8)
        return remote(o_ref.at[:, q], o_ref.at[:, q], e_s.at[k], e_r.at[k], sib)

    send_e0().start()

    def forward(k):
        send_d(k).wait()
        send_e(k).start()

    each(1, 8, forward)
    own_d.wait()
    send_e0().wait()
    each(1, 8, lambda k: send_e(k).wait())


def body(coeffs, src_pos, tgt_pos, interp):
    box = lax.axis_index("box")
    src = src_pos[0]
    ids = jnp.arange(64, dtype=jnp.int32)
    levels = jnp.arange(6, dtype=jnp.int32)
    same = (ids[None, :] >> levels[:, None]) == (box >> levels[:, None])
    sums = jnp.sum(jnp.where(same[:, :, None], src[None], 0), axis=1)
    row = jnp.concatenate([tgt_pos.reshape(64), sums.reshape(12), jnp.zeros((52,), jnp.int32)]).astype(F32)
    aux = jnp.broadcast_to(row[None, :], (8, 128))
    x = coeffs.reshape(2, 16, 16, 512)
    vm = pltpu.VMEM
    dma = pltpu.SemaphoreType.DMA
    result = pl.pallas_call(
        kernel,
        out_shape=jax.ShapeDtypeStruct((2, 16, 16, 512), F32),
        in_specs=[pl.BlockSpec(memory_space=pl.ANY)] * 3,
        out_specs=pl.BlockSpec(memory_space=pl.ANY),
        scratch_shapes=[
            vm((16, 8, 128), F32),
            vm((16, 16, 128), F32),
            vm((16, 128), F32),
            vm((16, 2, 16, 512), F32),
            vm((2, 512, 512), F32),
            vm((2, 2, 512, 256), BF16),
            vm((2, 2, 512, 256), BF16),
            vm((2, 16, 2, 16, 256), BF16),
            vm((2, 16, 2, 16, 256), BF16),
            vm((2, 16, 2, 16, 256), F32),
            vm((5, 2, 16, 256), F32),
            vm((3, 32, 2, 16, 256), F32),
            vm((16, 2, 8, 256), F32),
            vm((2, 4, 256, 128), F32),
            vm((16, 2, 4, 16, 128), F32),
            vm((16, 4, 8, 128), F32),
            vm((4, 128, 128), F32),
            vm((4, 2, 16, 512), F32),
            dma((16,)), dma((16,)), dma((16,)), dma((16,)), dma((16,)), dma((16,)), dma((16,)), dma((16,)),
            dma((16,)), dma((16,)), dma((8,)), dma((8,)), dma((8,)), dma((8,)), dma((8,)),
        ],
        compiler_params=pltpu.CompilerParams(collective_id=0, has_side_effects=True),
    )(x, aux, interp)
    return result.reshape(32, 16, 512)


def solution(mesh):
    in_specs = (P("angle", "box", None, None), P("angle", None, None), P("box", None), P())
    return jax.shard_map(body, mesh=mesh, in_specs=in_specs, out_specs=P("box", None, None), check_vma=False)
```

```python
import math

import jax
import jax.numpy as jnp
from jax import lax
from jax.experimental import pallas as pl
from jax.experimental.pallas import tpu as pltpu
from jax.sharding import PartitionSpec as P

MESH = pl.DeviceIdType.MESH
F32 = jnp.float32
BF16 = jnp.bfloat16
TWO_PI = 2.0 * math.pi


def cos_sin(turns):
    r = (turns - jnp.floor(turns + 0.5)) * math.pi
    x = r * r
    s = r * (2.0 + x * (-2.0 / 6 + x * (2.0 / 120 + x * (-2.0 / 5040 + x * (2.0 / 362880 + x * (-2.0 / 39916800))))))
    c = 1.0 + x * (
        -0.5 + x * (1.0 / 24 + x * (-1.0 / 720 + x * (1.0 / 40320 + x * (-1.0 / 3628800 + x * (1.0 / 479001600)))))
    )
    return 1.0 - 0.5 * (s * s), s * c


def split(value):
    hi = value.astype(BF16)
    lo = (value - hi.astype(F32)).astype(BF16)
    return hi, lo


def kernel(
    x_ref, src_ref, tgt_ref, w_ref, o_ref,
    srcv, tgtv, aux_o, aux_a, aux_b, auxf, ra, wf, whi, wlo, lhi, llo, out, tab1, tab2, tab5, bsend, brecv, csend, crecv,
    sa_s, sa_r, sx_s, sx_r, ba_s, ba_r, bx_s, bx_r, c_s, c_r, d_s, d_r, e_s, e_r, loc,
):
    box = lax.axis_index("box")
    ang = lax.axis_index("angle")
    xy = box // 4
    zlo = box % 4
    par = zlo % 2
    n = ang * 4 + zlo
    row = par * 8 + ang * 2 + zlo // 2
    core = ang % 2
    z8 = (ang // 2) * 4 + zlo

    def zdev(m):
        return {"box": xy * 4 + m % 4, "angle": m // 4}

    def xydev(m):
        return {"box": m * 4 + zlo, "angle": ang}

    def z8dev(m):
        return {"box": xy * 4 + m % 4, "angle": (m // 4) * 2 + core}

    sib = {"box": box, "angle": ang + 1 - 2 * core}

    def each(lo, hi, fn, un=1):
        def step(k, carry):
            for j in range(un):
                fn(lo + k * un + j)
            return carry

        lax.fori_loop(0, (hi - lo) // un, step, 0)

    def remote(src, dst, ss, rs, dev):
        return pltpu.make_async_remote_copy(src, dst, ss, rs, device_id=dev, device_id_type=MESH)

    barrier = pltpu.get_barrier_semaphore()
    each(1, 16, lambda k: pl.semaphore_signal(barrier, inc=1, device_id=zdev((n + k) % 16), device_id_type=MESH))
    each(1, 16, lambda k: pl.semaphore_signal(barrier, inc=1, device_id=xydev((xy + k) % 16), device_id_type=MESH))

    small = [pltpu.make_async_copy(src_ref, srcv, loc.at[2]), pltpu.make_async_copy(tgt_ref, tgtv, loc.at[3])]
    for copy in small:
        copy.start()
    wcopy = pltpu.make_async_copy(w_ref, wf, loc.at[0])
    wcopy.start()
    own_x = pltpu.make_async_copy(x_ref.at[:, n], ra.at[:, n], loc.at[1])
    own_x.start()
    for copy in small:
        copy.wait()
    lane2 = lax.broadcasted_iota(jnp.int32, (2, 128), 1)
    info = jnp.concatenate([tgtv[...].astype(F32), jnp.zeros((2, 96), F32)], axis=1)
    srcs = jnp.concatenate([srcv[...].astype(F32), jnp.zeros((2, 64), F32)], axis=1)
    for b in range(6):
        first = box // 2**b * 2**b
        total = jnp.sum(jnp.where((lane2 >= first) & (lane2 < first + 2**b), srcs, 0.0), axis=1, keepdims=True)
        info = jnp.where(lane2 == 32 + b, total, info)
    aux_o[...] = jnp.concatenate([info, jnp.zeros((6, 128), F32)], axis=0)
    own_aux = pltpu.make_async_copy(aux_o, aux_a.at[row], loc.at[2])
    own_aux.start()
    pl.semaphore_wait(barrier, 30)

    def send_aux_a(k):
        return remote(aux_o, aux_a.at[row], sa_s.at[k], sa_r.at[k], zdev((n + k) % 16))

    def send_a(h, k):
        m = (n + k) % 16
        return remote(x_ref.at[h, m], ra.at[h, n], sx_s.at[h, k], sx_r.at[h, k], zdev(m))

    each(1, 16, lambda k: send_aux_a(k).start())
    for h in range(2):
        each(1, 16, lambda k: send_a(h, k).start())

    wcopy.wait()
    for level in range(2):
        for t in range(2):
            hi, lo = split(wf[level, :, t * 256 : (t + 1) * 256])
            whi[level, t] = hi
            wlo[level, t] = lo

    own_aux.wait()
    each(1, 16, lambda k: send_aux_a(k).wait())
    for i in range(2):
        auxf[i] = jnp.concatenate([aux_a[r, i : i + 1, :] for r in range(16)], axis=0)
    own_auxb = pltpu.make_async_copy(auxf, aux_b.at[xy], loc.at[3])
    own_auxb.start()

    def send_aux_b(k):
        return remote(auxf, aux_b.at[xy], ba_s.at[k], ba_r.at[k], xydev((xy + k) % 16))

    each(1, 16, lambda k: send_aux_b(k).start())

    point = lax.broadcasted_iota(jnp.int32, (8, 256), 1)
    node_u, _ = cos_sin((2.0 * (point // 16).astype(F32) + 1.0) / 64.0)
    node_v, _ = cos_sin((2.0 * (point % 16).astype(F32) + 1.0) / 64.0)

    def tgt(ax, ay, t):
        hit = lax.broadcasted_iota(jnp.int32, ax.shape, 1) == t * 16 + n
        return [jnp.sum(jnp.where(hit, a, 0.0), axis=1, keepdims=True) for a in (ax, ay)]

    def src(ax, ay, b):
        return ax[:, 32 + b : 33 + b], ay[:, 32 + b : 33 + b]

    def phases(cu, cv):
        rows = cu.shape[0]
        cu = jnp.broadcast_to(cu, (rows, 256))
        cv = jnp.broadcast_to(cv, (rows, 256))
        u = jnp.concatenate([node_u] * (rows // 8), axis=0)
        v = jnp.concatenate([node_v] * (rows // 8), axis=0)
        return cos_sin(cu * u + cv * v)

    def ts(level):
        return 1.0 / (32.0 * (level + 1.0))

    def cs(level):
        return -1.0 / (32.0 * 2.0**level)

    ax, ay = auxf[0], auxf[1]
    s0 = src(ax, ay, 0)
    tab1[0, 0], tab1[0, 1] = phases(s0[0] * cs(0), s0[1] * cs(0))
    for t in range(2):
        tx, ty = tgt(ax, ay, t)
        for level in range(2):
            cx, cy = src(ax, ay, level + 1)
            c, s = phases(tx * ts(level) + cx * cs(level + 1), ty * ts(level) + cy * cs(level + 1))
            tab1[1 + 2 * level + t, 0], tab1[1 + 2 * level + t, 1] = c, s

    def table2(i):
        d, t = i // 2, i % 2
        ax, ay = aux_b[d, 0], aux_b[d, 1]
        tx, ty = tgt(ax, ay, t)
        for level in (2, 3, 4):
            cx, cy = src(ax, ay, level + 1)
            c, s = phases(tx * ts(level) + cx * cs(level + 1), ty * ts(level) + cy * cs(level + 1))
            tab2[level - 2, i, 0], tab2[level - 2, i, 1] = c, s

    srow = lax.broadcasted_iota(jnp.int32, (8, 128), 0)
    srow2 = lax.broadcasted_iota(jnp.int32, (8, 256), 0)

    def pick(rows, values):
        a, b, c, d = values
        return jnp.where(rows < 4, jnp.where(rows < 2, a, b), jnp.where(rows < 6, c, d))

    def table5(i):
        pp, h = i // 2, i % 2
        ax, ay = [
            pick(
                srow,
                [aux_b[2 * pp + p2 + 8 * h5, e, pl.ds(pl.multiple_of(h * 8, 8), 8), :] for p2 in range(2) for h5 in range(2)],
            )
            for e in range(2)
        ]
        for t in range(2):
            tx, ty = tgt(ax, ay, t)
            tab5[h, t, pp, 0], tab5[h, t, pp, 1] = phases(tx * ts(5), ty * ts(5))

    def rotated(re, im, c, s):
        return re * c - im * s, re * s + im * c

    def place(d, t, bit):
        stride = 1 << bit
        c = (d // stride) % 2
        return d - c * stride + t * stride, c

    def matmul(level, blocks):
        w = level % 2
        rows = blocks * 16
        for t in range(2):
            acc = None
            for c in range(2):
                h = lhi[c, 0:blocks].reshape(rows, 256)
                l = llo[c, 0:blocks].reshape(rows, 256)
                wh = whi[w, t, c * 256 : (c + 1) * 256, :]
                wl = wlo[w, t, c * 256 : (c + 1) * 256, :]
                for a, b in ((h, wh), (l, wh), (h, wl)):
                    p = jnp.dot(a, b, preferred_element_type=F32)
                    acc = p if acc is None else acc + p
            out[t, 0:blocks] = acc.reshape(blocks, 16, 256)

    def put(c, block, value):
        lhi[c, block], llo[c, block] = split(value)

    def levels01(h):
        def build0(i):
            j, b0 = i // 2, i % 2
            v = ra[h, (j // 2) * 4 + (j % 2) * 2 + b0]
            r = pl.ds(b0 * 8 + j, 1)
            re, im = rotated(v[:, 0:256], v[:, 256:512], tab1[0, 0, r, :], tab1[0, 1, r, :])
            put(b0, 2 * j, re)
            put(b0, 2 * j + 1, im)

        each(0, 16, build0, 4)
        matmul(0, 16)

        def build1(i):
            j, t = i // 2, i % 2
            r = pl.ds(h * 8 + j, 1)
            re, im = rotated(out[t, 2 * j], out[t, 2 * j + 1], tab1[1 + t, 0, r, :], tab1[1 + t, 1, r, :])
            b, c = place(j, t, 0)
            put(c, 2 * b, re)
            put(c, 2 * b + 1, im)

        each(0, 16, build1, 4)
        matmul(1, 16)

        def post1(i):
            j, t = i // 2, i % 2
            r = pl.ds(h * 8 + j, 1)
            re, im = rotated(out[t, 2 * j], out[t, 2 * j + 1], tab1[3 + t, 0, r, :], tab1[3 + t, 1, r, :])
            for cb, v in enumerate((re[:, 0:128], re[:, 128:256], im[:, 0:128], im[:, 128:256])):
                bsend[h, pl.ds((t * 4 + cb) * 8 + j, 16, stride=64), :] = v

        each(0, 16, post1, 4)

    def bchunk(h, f):
        return bsend.at[h, pl.ds(pl.multiple_of(f * 64, 64), 64), :]

    def own_b(h):
        return pltpu.make_async_copy(bchunk(h, xy), brecv.at[h, xy], loc.at[4 + h])

    def send_b(h, k):
        m = (xy + k) % 16
        return remote(bchunk(h, m), brecv.at[h, xy], bx_s.at[h, k], bx_r.at[h, k], xydev(m))

    def start_b(h):
        own_b(h).start()
        each(1, 16, lambda k: send_b(h, k).start())

    def wait_b(h):
        own_b(h).wait()
        each(1, 16, lambda k: send_b(h, k).wait())

    def levels25(h):
        half = slice(h * 8, h * 8 + 8)

        def build2(i):
            d, t = i // 2, i % 2
            v = [brecv[h, d, pl.ds(pl.multiple_of((t * 4 + cb) * 8, 8), 8), :] for cb in range(4)]
            j, c = place(d, t, 0)
            put(c, j, jnp.concatenate([jnp.concatenate(v[0:2], axis=1), jnp.concatenate(v[2:4], axis=1)], axis=0))

        each(0, 32, build2, 4)
        matmul(2, 16)
        for bit in (1, 2):

            def build34(i):
                d, t = i // 2, i % 2
                v = out[t, d]
                re, im = rotated(v[0:8], v[8:16], tab2[bit - 1, i, 0, half, :], tab2[bit - 1, i, 1, half, :])
                j, c = place(d, t, bit)
                put(c, j, jnp.concatenate([re, im], axis=0))

            each(0, 32, build34, 4)
            matmul(bit + 2, 16)

        def build5(i):
            pp, c = i // 2, i % 2
            sums = [[], []]
            for p2 in range(2):
                for t in range(2):
                    d = 2 * pp + p2 + 8 * c
                    v = out[t, d]
                    both = rotated(v[0:8], v[8:16], tab2[2, 2 * d + t, 0, half, :], tab2[2, 2 * d + t, 1, half, :])
                    for e in range(2):
                        w = both[e] + pltpu.roll(both[e], 4, 0)
                        sums[e].append(w + pltpu.roll(w, 2, 0))
            put(c, pp, jnp.concatenate([pick(srow2, sums[0]), pick(srow2, sums[1])], axis=0))

        each(0, 8, build5, 2)
        matmul(5, 4)

        for pp in range(4):
            for t in range(2):
                v = out[t, pp]
                re, im = rotated(v[0:8], v[8:16], tab5[h, t, pp, 0], tab5[h, t, pp, 1])
                for cb, w in enumerate((re[:, 0:128], re[:, 128:256], im[:, 0:128], im[:, 128:256])):
                    csend[h, pp * 8 : pp * 8 + 8, t * 4 + cb, :] = w

    def cchunk(h, d):
        return csend.at[h, pl.ds(((d % 8) // 2) * 8 + (d % 2) * 4 + (d // 8) * 2, 2)]

    def own_c(h):
        return pltpu.make_async_copy(cchunk(h, xy), crecv.at[h, :, xy], loc.at[6 + h])

    def send_c(h, k):
        m = (xy + k) % 16
        return remote(cchunk(h, m), crecv.at[h, :, xy], c_s.at[h, k], c_r.at[h, k], xydev(m))

    def start_c(h):
        own_c(h).start()
        each(1, 16, lambda k: send_c(h, k).start())

    def wait_c(h):
        own_c(h).wait()
        each(1, 16, lambda k: send_c(h, k).wait())

    own_q = o_ref.at[n]

    def send_d(k):
        m = (z8 + k) % 8
        return remote(crecv.at[m % 2, (m % 4) // 2], own_q, d_s.at[k], d_r.at[k], z8dev(m))

    own_d = pltpu.make_async_copy(crecv.at[par, zlo // 2], own_q, loc.at[8])

    def send_e0():
        return remote(crecv.at[par, zlo // 2], own_q, e_s.at[0], e_r.at[0], sib)

    def send_e(k):
        m = (z8 + 8 - k) % 8
        q = ((m // 4) * 2 + core) * 4 + m % 4
        return remote(o_ref.at[q], o_ref.at[q], e_s.at[k], e_r.at[k], sib)

    def start_d(h):
        def one(k):
            @pl.when((z8 + k) % 2 == h)
            def _():
                send_d(k).start()

        each(1, 8, one)

        @pl.when(par == h)
        def _():
            own_d.start()
            send_e0().start()

    own_x.wait()
    each(1, 16, lambda k: send_a(0, k).wait())
    levels01(0)
    start_b(0)
    own_auxb.wait()
    each(1, 16, lambda k: send_aux_b(k).wait())
    each(0, 32, table2, 2)
    each(0, 8, table5, 2)
    each(1, 16, lambda k: send_a(1, k).wait())
    levels01(1)
    start_b(1)
    wait_b(0)
    levels25(0)
    start_c(0)
    wait_b(1)
    levels25(1)
    start_c(1)
    wait_c(0)
    start_d(0)
    wait_c(1)
    start_d(1)

    def forward(k):
        send_d(k).wait()
        send_e(k).start()

    each(1, 8, forward)
    own_d.wait()
    send_e0().wait()
    each(1, 8, lambda k: send_e(k).wait())


def turn(i_ref, o_ref):
    for s in range(8):
        t, cb = s // 4, s % 4
        o_ref[t, 0, :, cb * 128 : cb * 128 + 128] = i_ref[0, :, s, :]


def body(coeffs, src_pos, tgt_pos, interp):
    x = coeffs.reshape(2, 16, 16, 512)
    vm = pltpu.VMEM
    dma = pltpu.SemaphoreType.DMA
    gathered = pl.pallas_call(
        kernel,
        out_shape=jax.ShapeDtypeStruct((16, 16, 8, 128), F32),
        in_specs=[pl.BlockSpec(memory_space=pl.ANY)] * 4,
        out_specs=pl.BlockSpec(memory_space=pl.ANY),
        scratch_shapes=[
            vm((2, 64), jnp.int32),
            vm((2, 32), jnp.int32),
            vm((8, 128), F32),
            vm((16, 8, 128), F32),
            vm((16, 2, 16, 128), F32),
            vm((2, 16, 128), F32),
            vm((2, 16, 16, 512), F32),
            vm((2, 512, 512), F32),
            vm((2, 2, 512, 256), BF16),
            vm((2, 2, 512, 256), BF16),
            vm((2, 16, 16, 256), BF16),
            vm((2, 16, 16, 256), BF16),
            vm((2, 16, 16, 256), F32),
            vm((5, 2, 16, 256), F32),
            vm((3, 32, 2, 16, 256), F32),
            vm((2, 2, 4, 2, 8, 256), F32),
            vm((2, 1024, 128), F32),
            vm((2, 16, 64, 128), F32),
            vm((2, 32, 8, 128), F32),
            vm((2, 2, 16, 8, 128), F32),
            dma((16,)), dma((16,)), dma((2, 16)), dma((2, 16)), dma((16,)), dma((16,)), dma((2, 16)), dma((2, 16)),
            dma((2, 16)), dma((2, 16)), dma((8,)), dma((8,)), dma((8,)), dma((8,)), dma((9,)),
        ],
        compiler_params=pltpu.CompilerParams(collective_id=0, has_side_effects=True),
    )(x, src_pos[0].T, tgt_pos.T, interp)
    result = pl.pallas_call(
        turn,
        out_shape=jax.ShapeDtypeStruct((2, 16, 16, 512), F32),
        grid=(16,),
        in_specs=[pl.BlockSpec((1, 16, 8, 128), lambda q: (q, 0, 0, 0))],
        out_specs=pl.BlockSpec((2, 1, 16, 512), lambda q: (0, q, 0, 0)),
    )(gathered)
    return result.reshape(32, 16, 512)


def solution(mesh):
    in_specs = (P("angle", "box", None, None), P("angle", None, None), P("box", None), P())
    return jax.shard_map(body, mesh=mesh, in_specs=in_specs, out_specs=P("box", None, None), check_vma=False)
```

```python
import math

import jax
import jax.numpy as jnp
from jax import lax
from jax.experimental import pallas as pl
from jax.experimental.pallas import tpu as pltpu
from jax.sharding import PartitionSpec as P

MESH = pl.DeviceIdType.MESH
F32 = jnp.float32
BF16 = jnp.bfloat16
TWO_PI = 2.0 * math.pi


def cos_sin(turns):
    r = (turns - jnp.floor(turns + 0.5)) * math.pi
    x = r * r
    s = r * (2.0 + x * (-2.0 / 6 + x * (2.0 / 120 + x * (-2.0 / 5040 + x * (2.0 / 362880 + x * (-2.0 / 39916800))))))
    c = 1.0 + x * (
        -0.5 + x * (1.0 / 24 + x * (-1.0 / 720 + x * (1.0 / 40320 + x * (-1.0 / 3628800 + x * (1.0 / 479001600)))))
    )
    return 1.0 - 0.5 * (s * s), s * c


def split(value):
    hi = value.astype(BF16)
    lo = (value - hi.astype(F32)).astype(BF16)
    return hi, lo


def kernel(
    x_ref, src_ref, tgt_ref, w_ref, o_ref,
    srcv, tgtv, aux_o, aux_a, aux_b, auxf, ra, wf, whi, wlo, lhi, llo, out, tab1, tab2, tab5, bsend, brecv, csend, crecv, drecv,
    sa_s, sa_r, sx_s, sx_r, ba_s, ba_r, bx_s, bx_r, c_s, c_r, d_s, d_r, e_s, e_r, loc,
):
    box = lax.axis_index("box")
    ang = lax.axis_index("angle")
    xy = box // 4
    zlo = box % 4
    par = zlo % 2
    n = ang * 4 + zlo
    row = par * 8 + ang * 2 + zlo // 2
    core = ang % 2
    z8 = (ang // 2) * 4 + zlo

    def zdev(m):
        return {"box": xy * 4 + m % 4, "angle": m // 4}

    def xydev(m):
        return {"box": m * 4 + zlo, "angle": ang}

    def z8dev(m):
        return {"box": xy * 4 + m % 4, "angle": (m // 4) * 2 + core}

    sib = {"box": box, "angle": ang + 1 - 2 * core}

    def each(lo, hi, fn, un=1):
        def step(k, carry):
            for j in range(un):
                fn(lo + k * un + j)
            return carry

        lax.fori_loop(0, (hi - lo) // un, step, 0)

    def remote(src, dst, ss, rs, dev):
        return pltpu.make_async_remote_copy(src, dst, ss, rs, device_id=dev, device_id_type=MESH)

    barrier = pltpu.get_barrier_semaphore()
    each(1, 16, lambda k: pl.semaphore_signal(barrier, inc=1, device_id=zdev((n + k) % 16), device_id_type=MESH))
    each(1, 16, lambda k: pl.semaphore_signal(barrier, inc=1, device_id=xydev((xy + k) % 16), device_id_type=MESH))

    small = [pltpu.make_async_copy(src_ref, srcv, loc.at[2]), pltpu.make_async_copy(tgt_ref, tgtv, loc.at[3])]
    for copy in small:
        copy.start()
    wcopy = pltpu.make_async_copy(w_ref, wf, loc.at[0])
    wcopy.start()
    own_x = pltpu.make_async_copy(x_ref.at[:, n], ra.at[:, n], loc.at[1])
    own_x.start()
    for copy in small:
        copy.wait()
    lane2 = lax.broadcasted_iota(jnp.int32, (2, 128), 1)
    info = jnp.concatenate([tgtv[...].astype(F32), jnp.zeros((2, 96), F32)], axis=1)
    srcs = jnp.concatenate([srcv[...].astype(F32), jnp.zeros((2, 64), F32)], axis=1)
    for b in range(6):
        first = box // 2**b * 2**b
        total = jnp.sum(jnp.where((lane2 >= first) & (lane2 < first + 2**b), srcs, 0.0), axis=1, keepdims=True)
        info = jnp.where(lane2 == 32 + b, total, info)
    aux_o[...] = jnp.concatenate([info, jnp.zeros((6, 128), F32)], axis=0)
    own_aux = pltpu.make_async_copy(aux_o, aux_a.at[row], loc.at[2])
    own_aux.start()
    pl.semaphore_wait(barrier, 30)

    def send_aux_a(k):
        return remote(aux_o, aux_a.at[row], sa_s.at[k], sa_r.at[k], zdev((n + k) % 16))

    def send_a(h, k):
        m = (n + k) % 16
        return remote(x_ref.at[h, m], ra.at[h, n], sx_s.at[h, k], sx_r.at[h, k], zdev(m))

    each(1, 16, lambda k: send_aux_a(k).start())
    for h in range(2):
        each(1, 16, lambda k: send_a(h, k).start())

    wcopy.wait()
    for level in range(2):
        for t in range(2):
            hi, lo = split(wf[level, :, t * 256 : (t + 1) * 256])
            whi[level, t] = hi
            wlo[level, t] = lo

    own_aux.wait()
    each(1, 16, lambda k: send_aux_a(k).wait())
    for i in range(2):
        auxf[i] = jnp.concatenate([aux_a[r, i : i + 1, :] for r in range(16)], axis=0)
    own_auxb = pltpu.make_async_copy(auxf, aux_b.at[xy], loc.at[3])
    own_auxb.start()

    def send_aux_b(k):
        return remote(auxf, aux_b.at[xy], ba_s.at[k], ba_r.at[k], xydev((xy + k) % 16))

    each(1, 16, lambda k: send_aux_b(k).start())

    point = lax.broadcasted_iota(jnp.int32, (8, 256), 1)
    node_u, _ = cos_sin((2.0 * (point // 16).astype(F32) + 1.0) / 64.0)
    node_v, _ = cos_sin((2.0 * (point % 16).astype(F32) + 1.0) / 64.0)

    def tgt(ax, ay, t):
        hit = lax.broadcasted_iota(jnp.int32, ax.shape, 1) == t * 16 + n
        return [jnp.sum(jnp.where(hit, a, 0.0), axis=1, keepdims=True) for a in (ax, ay)]

    def src(ax, ay, b):
        return ax[:, 32 + b : 33 + b], ay[:, 32 + b : 33 + b]

    def phases(cu, cv):
        rows = cu.shape[0]
        cu = jnp.broadcast_to(cu, (rows, 256))
        cv = jnp.broadcast_to(cv, (rows, 256))
        u = jnp.concatenate([node_u] * (rows // 8), axis=0)
        v = jnp.concatenate([node_v] * (rows // 8), axis=0)
        return cos_sin(cu * u + cv * v)

    def ts(level):
        return 1.0 / (32.0 * (level + 1.0))

    def cs(level):
        return -1.0 / (32.0 * 2.0**level)

    ax, ay = auxf[0], auxf[1]
    s0 = src(ax, ay, 0)
    tab1[0, 0], tab1[0, 1] = phases(s0[0] * cs(0), s0[1] * cs(0))
    for t in range(2):
        tx, ty = tgt(ax, ay, t)
        for level in range(2):
            cx, cy = src(ax, ay, level + 1)
            c, s = phases(tx * ts(level) + cx * cs(level + 1), ty * ts(level) + cy * cs(level + 1))
            tab1[1 + 2 * level + t, 0], tab1[1 + 2 * level + t, 1] = c, s

    def table2(i):
        d, t = i // 2, i % 2
        ax, ay = aux_b[d, 0], aux_b[d, 1]
        tx, ty = tgt(ax, ay, t)
        for level in (2, 3, 4):
            cx, cy = src(ax, ay, level + 1)
            c, s = phases(tx * ts(level) + cx * cs(level + 1), ty * ts(level) + cy * cs(level + 1))
            tab2[level - 2, i, 0], tab2[level - 2, i, 1] = c, s

    srow = lax.broadcasted_iota(jnp.int32, (8, 128), 0)
    srow2 = lax.broadcasted_iota(jnp.int32, (8, 256), 0)

    def pick(rows, values):
        a, b, c, d = values
        return jnp.where(rows < 4, jnp.where(rows < 2, a, b), jnp.where(rows < 6, c, d))

    def table5(i):
        pp, h = i // 2, i % 2
        ax, ay = [
            pick(
                srow,
                [aux_b[2 * pp + p2 + 8 * h5, e, pl.ds(pl.multiple_of(h * 8, 8), 8), :] for p2 in range(2) for h5 in range(2)],
            )
            for e in range(2)
        ]
        for t in range(2):
            tx, ty = tgt(ax, ay, t)
            tab5[h, t, pp, 0], tab5[h, t, pp, 1] = phases(tx * ts(5), ty * ts(5))

    def rotated(re, im, c, s):
        return re * c - im * s, re * s + im * c

    def place(d, t, bit):
        stride = 1 << bit
        c = (d // stride) % 2
        return d - c * stride + t * stride, c

    def matmul(level, blocks):
        w = level % 2
        rows = blocks * 16
        for t in range(2):
            acc = None
            for c in range(2):
                h = lhi[c, 0:blocks].reshape(rows, 256)
                l = llo[c, 0:blocks].reshape(rows, 256)
                wh = whi[w, t, c * 256 : (c + 1) * 256, :]
                wl = wlo[w, t, c * 256 : (c + 1) * 256, :]
                for a, b in ((h, wh), (l, wh), (h, wl)):
                    p = jnp.dot(a, b, preferred_element_type=F32)
                    acc = p if acc is None else acc + p
            out[t, 0:blocks] = acc.reshape(blocks, 16, 256)

    def put(c, block, value):
        lhi[c, block], llo[c, block] = split(value)

    def levels01(h):
        def build0(i):
            j, b0 = i // 2, i % 2
            v = ra[h, (j // 2) * 4 + (j % 2) * 2 + b0]
            r = pl.ds(b0 * 8 + j, 1)
            re, im = rotated(v[:, 0:256], v[:, 256:512], tab1[0, 0, r, :], tab1[0, 1, r, :])
            put(b0, 2 * j, re)
            put(b0, 2 * j + 1, im)

        each(0, 16, build0, 4)
        matmul(0, 16)

        def build1(i):
            j, t = i // 2, i % 2
            r = pl.ds(h * 8 + j, 1)
            re, im = rotated(out[t, 2 * j], out[t, 2 * j + 1], tab1[1 + t, 0, r, :], tab1[1 + t, 1, r, :])
            b, c = place(j, t, 0)
            put(c, 2 * b, re)
            put(c, 2 * b + 1, im)

        each(0, 16, build1, 4)
        matmul(1, 16)

        def post1(i):
            j, t = i // 2, i % 2
            r = pl.ds(h * 8 + j, 1)
            re, im = rotated(out[t, 2 * j], out[t, 2 * j + 1], tab1[3 + t, 0, r, :], tab1[3 + t, 1, r, :])
            for cb, v in enumerate((re[:, 0:128], re[:, 128:256], im[:, 0:128], im[:, 128:256])):
                bsend[h, pl.ds((t * 4 + cb) * 8 + j, 16, stride=64), :] = v

        each(0, 16, post1, 4)

    def bchunk(h, f):
        return bsend.at[h, pl.ds(pl.multiple_of(f * 64, 64), 64), :]

    def own_b(h):
        return pltpu.make_async_copy(bchunk(h, xy), brecv.at[h, xy], loc.at[4 + h])

    def send_b(h, k):
        m = (xy + k) % 16
        return remote(bchunk(h, m), brecv.at[h, xy], bx_s.at[h, k], bx_r.at[h, k], xydev(m))

    def start_b(h):
        own_b(h).start()
        each(1, 16, lambda k: send_b(h, k).start())

    def wait_b(h):
        own_b(h).wait()
        each(1, 16, lambda k: send_b(h, k).wait())

    def levels25(h):
        half = slice(h * 8, h * 8 + 8)

        def build2(i):
            d, t = i // 2, i % 2
            v = [brecv[h, d, pl.ds(pl.multiple_of((t * 4 + cb) * 8, 8), 8), :] for cb in range(4)]
            j, c = place(d, t, 0)
            put(c, j, jnp.concatenate([jnp.concatenate(v[0:2], axis=1), jnp.concatenate(v[2:4], axis=1)], axis=0))

        each(0, 32, build2, 4)
        matmul(2, 16)
        for bit in (1, 2):

            def build34(i):
                d, t = i // 2, i % 2
                v = out[t, d]
                re, im = rotated(v[0:8], v[8:16], tab2[bit - 1, i, 0, half, :], tab2[bit - 1, i, 1, half, :])
                j, c = place(d, t, bit)
                put(c, j, jnp.concatenate([re, im], axis=0))

            each(0, 32, build34, 4)
            matmul(bit + 2, 16)

        def build5(i):
            pp, c = i // 2, i % 2
            sums = [[], []]
            for p2 in range(2):
                for t in range(2):
                    d = 2 * pp + p2 + 8 * c
                    v = out[t, d]
                    both = rotated(v[0:8], v[8:16], tab2[2, 2 * d + t, 0, half, :], tab2[2, 2 * d + t, 1, half, :])
                    for e in range(2):
                        w = both[e] + pltpu.roll(both[e], 4, 0)
                        sums[e].append(w + pltpu.roll(w, 2, 0))
            put(c, pp, jnp.concatenate([pick(srow2, sums[0]), pick(srow2, sums[1])], axis=0))

        each(0, 8, build5, 2)
        matmul(5, 4)

        for pp in range(4):
            for t in range(2):
                v = out[t, pp]
                re, im = rotated(v[0:8], v[8:16], tab5[h, t, pp, 0], tab5[h, t, pp, 1])
                for cb, w in enumerate((re[:, 0:128], re[:, 128:256], im[:, 0:128], im[:, 128:256])):
                    csend[h, pp * 8 : pp * 8 + 8, t * 4 + cb, :] = w

    def cchunk(h, d):
        return csend.at[h, pl.ds(((d % 8) // 2) * 8 + (d % 2) * 4 + (d // 8) * 2, 2)]

    def own_c(h):
        return pltpu.make_async_copy(cchunk(h, xy), crecv.at[h, :, xy], loc.at[6 + h])

    def send_c(h, k):
        m = (xy + k) % 16
        return remote(cchunk(h, m), crecv.at[h, :, xy], c_s.at[h, k], c_r.at[h, k], xydev(m))

    def start_c(h):
        own_c(h).start()
        each(1, 16, lambda k: send_c(h, k).start())

    def wait_c(h):
        own_c(h).wait()
        each(1, 16, lambda k: send_c(h, k).wait())

    own_q = drecv.at[n]

    def send_d(k):
        m = (z8 + k) % 8
        return remote(crecv.at[m % 2, (m % 4) // 2], own_q, d_s.at[k], d_r.at[k], z8dev(m))

    own_d = pltpu.make_async_copy(crecv.at[par, zlo // 2], own_q, loc.at[8])

    def send_e0():
        return remote(crecv.at[par, zlo // 2], own_q, e_s.at[0], e_r.at[0], sib)

    def send_e(k):
        m = (z8 + 8 - k) % 8
        q = ((m // 4) * 2 + core) * 4 + m % 4
        return remote(drecv.at[q], drecv.at[q], e_s.at[k], e_r.at[k], sib)

    def turn(k, side):
        m = (z8 + 8 - k) % 8
        q = ((m // 4) * 2 + side) * 4 + m % 4
        for s in range(8):
            o_ref[s // 4, q, :, (s % 4) * 128 : (s % 4) * 128 + 128] = drecv[q, :, s, :]

    def start_d(h):
        def one(k):
            @pl.when((z8 + k) % 2 == h)
            def _():
                send_d(k).start()

        each(1, 8, one)

        @pl.when(par == h)
        def _():
            own_d.start()
            send_e0().start()

    own_x.wait()
    each(1, 16, lambda k: send_a(0, k).wait())
    levels01(0)
    start_b(0)
    own_auxb.wait()
    each(1, 16, lambda k: send_aux_b(k).wait())
    each(0, 32, table2, 2)
    each(0, 8, table5, 2)
    each(1, 16, lambda k: send_a(1, k).wait())
    levels01(1)
    start_b(1)
    wait_b(0)
    levels25(0)
    start_c(0)
    wait_b(1)
    levels25(1)
    start_c(1)
    wait_c(0)
    start_d(0)
    wait_c(1)
    start_d(1)

    def forward(k):
        send_d(k).wait()
        send_e(k).start()
        turn(k, core)

    own_d.wait()
    turn(0, core)
    each(1, 8, forward)
    send_e0().wait()
    turn(0, 1 - core)

    def last(k):
        send_e(k).wait()
        turn(k, 1 - core)

    each(1, 8, last)


def body(coeffs, src_pos, tgt_pos, interp):
    x = coeffs.reshape(2, 16, 16, 512)
    vm = pltpu.VMEM
    dma = pltpu.SemaphoreType.DMA
    result = pl.pallas_call(
        kernel,
        out_shape=pltpu.VMEM((2, 16, 16, 512), F32),
        in_specs=[pl.BlockSpec(memory_space=pl.ANY)] * 4,
        out_specs=pl.BlockSpec(memory_space=pltpu.VMEM),
        scratch_shapes=[
            vm((2, 64), jnp.int32),
            vm((2, 32), jnp.int32),
            vm((8, 128), F32),
            vm((16, 8, 128), F32),
            vm((16, 2, 16, 128), F32),
            vm((2, 16, 128), F32),
            vm((2, 16, 16, 512), F32),
            vm((2, 512, 512), F32),
            vm((2, 2, 512, 256), BF16),
            vm((2, 2, 512, 256), BF16),
            vm((2, 16, 16, 256), BF16),
            vm((2, 16, 16, 256), BF16),
            vm((2, 16, 16, 256), F32),
            vm((5, 2, 16, 256), F32),
            vm((3, 32, 2, 16, 256), F32),
            vm((2, 2, 4, 2, 8, 256), F32),
            vm((2, 1024, 128), F32),
            vm((2, 16, 64, 128), F32),
            vm((2, 32, 8, 128), F32),
            vm((2, 2, 16, 8, 128), F32),
            vm((16, 16, 8, 128), F32),
            dma((16,)), dma((16,)), dma((2, 16)), dma((2, 16)), dma((16,)), dma((16,)), dma((2, 16)), dma((2, 16)),
            dma((2, 16)), dma((2, 16)), dma((8,)), dma((8,)), dma((8,)), dma((8,)), dma((9,)),
        ],
        compiler_params=pltpu.CompilerParams(collective_id=0, has_side_effects=True),
    )(x, src_pos[0].T, tgt_pos.T, interp)
    return result.reshape(32, 16, 512)


def solution(mesh):
    in_specs = (P("angle", "box", None, None), P("angle", None, None), P("box", None), P())
    return jax.shard_map(body, mesh=mesh, in_specs=in_specs, out_specs=P("box", None, None), check_vma=False)
```

```python
import math

import jax
import jax.numpy as jnp
from jax import lax
from jax.experimental import pallas as pl
from jax.experimental.pallas import tpu as pltpu
from jax.sharding import PartitionSpec as P

MESH = pl.DeviceIdType.MESH
F32 = jnp.float32
BF16 = jnp.bfloat16
TWO_PI = 2.0 * math.pi


def cos_sin(turns):
    r = (turns - jnp.floor(turns + 0.5)) * math.pi
    x = r * r
    s = r * (2.0 + x * (-2.0 / 6 + x * (2.0 / 120 + x * (-2.0 / 5040 + x * (2.0 / 362880 + x * (-2.0 / 39916800))))))
    c = 1.0 + x * (
        -0.5 + x * (1.0 / 24 + x * (-1.0 / 720 + x * (1.0 / 40320 + x * (-1.0 / 3628800 + x * (1.0 / 479001600)))))
    )
    return 1.0 - 0.5 * (s * s), s * c


def split(value):
    hi = value.astype(BF16)
    lo = (value - hi.astype(F32)).astype(BF16)
    return hi, lo


def kernel(
    x_ref, src_ref, tgt_ref, w_ref, o_ref,
    srcv, tgtv, aux_o, aux_a, aux_b, auxf, ra, wf, whi, wlo, lhi, llo, out, tab1, tab2, tab5, bsend, brecv, csend, crecv, drecv,
    sa_s, sa_r, sx_s, sx_r, ba_s, ba_r, bx_s, bx_r, c_s, c_r, d_s, d_r, e_s, e_r, loc,
):
    box = lax.axis_index("box")
    ang = lax.axis_index("angle")
    xy = box // 4
    zlo = box % 4
    par = zlo % 2
    n = ang * 4 + zlo
    row = par * 8 + ang * 2 + zlo // 2
    core = ang % 2
    z8 = (ang // 2) * 4 + zlo

    def zdev(m):
        return {"box": xy * 4 + m % 4, "angle": m // 4}

    def xydev(m):
        return {"box": m * 4 + zlo, "angle": ang}

    def z8dev(m):
        return {"box": xy * 4 + m % 4, "angle": (m // 4) * 2 + core}

    sib = {"box": box, "angle": ang + 1 - 2 * core}

    def each(lo, hi, fn, un=1):
        def step(k, carry):
            for j in range(un):
                fn(lo + k * un + j)
            return carry

        lax.fori_loop(0, (hi - lo) // un, step, 0)

    def remote(src, dst, ss, rs, dev):
        return pltpu.make_async_remote_copy(src, dst, ss, rs, device_id=dev, device_id_type=MESH)

    barrier = pltpu.get_barrier_semaphore()
    each(1, 16, lambda k: pl.semaphore_signal(barrier, inc=1, device_id=zdev((n + k) % 16), device_id_type=MESH))
    each(1, 16, lambda k: pl.semaphore_signal(barrier, inc=1, device_id=xydev((xy + k) % 16), device_id_type=MESH))

    small = [pltpu.make_async_copy(src_ref, srcv, loc.at[2]), pltpu.make_async_copy(tgt_ref, tgtv, loc.at[3])]
    for copy in small:
        copy.start()
    wcopy = pltpu.make_async_copy(w_ref, wf, loc.at[0])
    wcopy.start()
    own_x = pltpu.make_async_copy(x_ref.at[:, n], ra.at[:, n], loc.at[1])
    own_x.start()
    for copy in small:
        copy.wait()
    lane2 = lax.broadcasted_iota(jnp.int32, (2, 128), 1)
    info = jnp.concatenate([tgtv[...].astype(F32), jnp.zeros((2, 96), F32)], axis=1)
    srcs = jnp.concatenate([srcv[...].astype(F32), jnp.zeros((2, 64), F32)], axis=1)
    for b in range(6):
        first = box // 2**b * 2**b
        total = jnp.sum(jnp.where((lane2 >= first) & (lane2 < first + 2**b), srcs, 0.0), axis=1, keepdims=True)
        info = jnp.where(lane2 == 32 + b, total, info)
    aux_o[...] = jnp.concatenate([info, jnp.zeros((6, 128), F32)], axis=0)
    own_aux = pltpu.make_async_copy(aux_o, aux_a.at[row], loc.at[2])
    own_aux.start()
    pl.semaphore_wait(barrier, 30)

    def send_aux_a(k):
        return remote(aux_o, aux_a.at[row], sa_s.at[k], sa_r.at[k], zdev((n + k) % 16))

    def send_a(h, k):
        m = (n + k) % 16
        return remote(x_ref.at[h, m], ra.at[h, n], sx_s.at[h, k], sx_r.at[h, k], zdev(m))

    each(1, 16, lambda k: send_aux_a(k).start())
    for h in range(2):
        each(1, 16, lambda k: send_a(h, k).start())

    wcopy.wait()
    for level in range(2):
        for t in range(2):
            hi, lo = split(wf[level, :, t * 256 : (t + 1) * 256])
            whi[level, t] = hi
            wlo[level, t] = lo

    own_aux.wait()
    each(1, 16, lambda k: send_aux_a(k).wait())
    for i in range(2):
        auxf[i] = jnp.concatenate([aux_a[r, i : i + 1, :] for r in range(16)], axis=0)
    own_auxb = pltpu.make_async_copy(auxf, aux_b.at[xy], loc.at[3])
    own_auxb.start()

    def send_aux_b(k):
        return remote(auxf, aux_b.at[xy], ba_s.at[k], ba_r.at[k], xydev((xy + k) % 16))

    each(1, 16, lambda k: send_aux_b(k).start())

    point = lax.broadcasted_iota(jnp.int32, (8, 256), 1)
    node_u, _ = cos_sin((2.0 * (point // 16).astype(F32) + 1.0) / 64.0)
    node_v, _ = cos_sin((2.0 * (point % 16).astype(F32) + 1.0) / 64.0)

    def tgt(ax, ay, t):
        hit = lax.broadcasted_iota(jnp.int32, ax.shape, 1) == t * 16 + n
        return [jnp.sum(jnp.where(hit, a, 0.0), axis=1, keepdims=True) for a in (ax, ay)]

    def src(ax, ay, b):
        return ax[:, 32 + b : 33 + b], ay[:, 32 + b : 33 + b]

    def phases(cu, cv):
        rows = cu.shape[0]
        cu = jnp.broadcast_to(cu, (rows, 256))
        cv = jnp.broadcast_to(cv, (rows, 256))
        u = jnp.concatenate([node_u] * (rows // 8), axis=0)
        v = jnp.concatenate([node_v] * (rows // 8), axis=0)
        return cos_sin(cu * u + cv * v)

    def ts(level):
        return 1.0 / (32.0 * (level + 1.0))

    def cs(level):
        return -1.0 / (32.0 * 2.0**level)

    ax, ay = auxf[0], auxf[1]
    s0 = src(ax, ay, 0)
    tab1[0, 0], tab1[0, 1] = phases(s0[0] * cs(0), s0[1] * cs(0))
    for t in range(2):
        tx, ty = tgt(ax, ay, t)
        for level in range(2):
            cx, cy = src(ax, ay, level + 1)
            c, s = phases(tx * ts(level) + cx * cs(level + 1), ty * ts(level) + cy * cs(level + 1))
            tab1[1 + 2 * level + t, 0], tab1[1 + 2 * level + t, 1] = c, s

    def table2(i):
        d, t = i // 2, i % 2
        ax, ay = aux_b[d, 0], aux_b[d, 1]
        tx, ty = tgt(ax, ay, t)
        for level in (2, 3, 4):
            cx, cy = src(ax, ay, level + 1)
            c, s = phases(tx * ts(level) + cx * cs(level + 1), ty * ts(level) + cy * cs(level + 1))
            tab2[level - 2, i, 0], tab2[level - 2, i, 1] = c, s

    srow = lax.broadcasted_iota(jnp.int32, (8, 128), 0)
    srow2 = lax.broadcasted_iota(jnp.int32, (8, 256), 0)

    def pick(rows, values):
        a, b, c, d = values
        return jnp.where(rows < 4, jnp.where(rows < 2, a, b), jnp.where(rows < 6, c, d))

    def table5(i):
        pp, h = i // 2, i % 2
        ax, ay = [
            pick(
                srow,
                [aux_b[4 * (pp % 2) + 2 * p2 + 8 * h5 + pp // 2, e, pl.ds(pl.multiple_of(h * 8, 8), 8), :] for p2 in range(2) for h5 in range(2)],
            )
            for e in range(2)
        ]
        for t in range(2):
            tx, ty = tgt(ax, ay, t)
            tab5[h, t, pp, 0], tab5[h, t, pp, 1] = phases(tx * ts(5), ty * ts(5))

    def rotated(re, im, c, s):
        return re * c - im * s, re * s + im * c

    def place(d, t, bit):
        stride = 1 << bit
        c = (d // stride) % 2
        return d - c * stride + t * stride, c

    def matmul(level, blocks, sides=(0, 1)):
        w = level % 2
        rows = blocks * 16
        for t in sides:
            acc = None
            for c in range(2):
                h = lhi[c, 0:blocks].reshape(rows, 256)
                l = llo[c, 0:blocks].reshape(rows, 256)
                wh = whi[w, t, c * 256 : (c + 1) * 256, :]
                wl = wlo[w, t, c * 256 : (c + 1) * 256, :]
                for a, b in ((h, wh), (l, wh), (h, wl)):
                    p = jnp.dot(a, b, preferred_element_type=F32)
                    acc = p if acc is None else acc + p
            out[t, 0:blocks] = acc.reshape(blocks, 16, 256)

    def put(c, block, value):
        lhi[c, block], llo[c, block] = split(value)

    def levels01(h):
        def build0(i):
            j, b0 = i // 2, i % 2
            v = ra[h, (j // 2) * 4 + (j % 2) * 2 + b0]
            r = pl.ds(b0 * 8 + j, 1)
            re, im = rotated(v[:, 0:256], v[:, 256:512], tab1[0, 0, r, :], tab1[0, 1, r, :])
            put(b0, 2 * j, re)
            put(b0, 2 * j + 1, im)

        each(0, 16, build0, 4)
        matmul(0, 16)

        def build1(i):
            j, t = i // 2, i % 2
            r = pl.ds(h * 8 + j, 1)
            re, im = rotated(out[t, 2 * j], out[t, 2 * j + 1], tab1[1 + t, 0, r, :], tab1[1 + t, 1, r, :])
            b, c = place(j, t, 0)
            put(c, 2 * b, re)
            put(c, 2 * b + 1, im)

        each(0, 16, build1, 4)
        for t in range(2):
            matmul(1, 16, (t,))

            def post1(j):
                r = pl.ds(h * 8 + j, 1)
                re, im = rotated(out[t, 2 * j], out[t, 2 * j + 1], tab1[3 + t, 0, r, :], tab1[3 + t, 1, r, :])
                for cb, v in enumerate((re[:, 0:128], re[:, 128:256], im[:, 0:128], im[:, 128:256])):
                    bsend[h, t, pl.ds(cb * 8 + j, 16, stride=32), :] = v

            each(0, 8, post1, 4)
            start_b(h, t)

    def bchunk(h, t, f):
        return bsend.at[h, t, pl.ds(pl.multiple_of(f * 32, 32), 32), :]

    def own_b(h, t):
        return pltpu.make_async_copy(bchunk(h, t, xy), brecv.at[h, t, xy], loc.at[4 + 2 * h + t])

    def send_b(h, t, k):
        m = (xy + k) % 16
        return remote(bchunk(h, t, m), brecv.at[h, t, xy], bx_s.at[h, t, k], bx_r.at[h, t, k], xydev(m))

    def start_b(h, t):
        own_b(h, t).start()
        each(1, 16, lambda k: send_b(h, t, k).start())

    def wait_b(h, t):
        own_b(h, t).wait()
        each(1, 16, lambda k: send_b(h, t, k).wait())

    def levels25(h, g):
        half = slice(h * 8, h * 8 + 8)

        def build2(d):
            v = [brecv[h, g, d, cb * 8 : cb * 8 + 8, :] for cb in range(4)]
            put(d % 2, d // 2, jnp.concatenate([jnp.concatenate(v[0:2], axis=1), jnp.concatenate(v[2:4], axis=1)], axis=0))

        each(0, 16, build2, 4)
        matmul(2, 8)
        for bit in (0, 1):

            def build34(i):
                j, t = i // 2, i % 2
                v = out[t, j]
                r = 4 * j + 2 * g + t
                re, im = rotated(v[0:8], v[8:16], tab2[bit, r, 0, half, :], tab2[bit, r, 1, half, :])
                b, c = place(j, t, bit)
                put(c, b, jnp.concatenate([re, im], axis=0))

            each(0, 16, build34, 4)
            matmul(bit + 3, 8)

        def build5(i):
            pp, c = i // 2, i % 2
            sums = [[], []]
            for p2 in range(2):
                for t in range(2):
                    j = 2 * pp + p2 + 4 * c
                    v = out[t, j]
                    r = 4 * j + 2 * g + t
                    both = rotated(v[0:8], v[8:16], tab2[2, r, 0, half, :], tab2[2, r, 1, half, :])
                    for e in range(2):
                        w = both[e] + pltpu.roll(both[e], 4, 0)
                        sums[e].append(w + pltpu.roll(w, 2, 0))
            put(c, pp, jnp.concatenate([pick(srow2, sums[0]), pick(srow2, sums[1])], axis=0))

        each(0, 4, build5, 4)
        matmul(5, 2)

        for pp in range(2):
            gp = g * 2 + pp
            for t in range(2):
                v = out[t, pp]
                re, im = rotated(v[0:8], v[8:16], tab5[h, t, gp, 0], tab5[h, t, gp, 1])
                for cb, w in enumerate((re[:, 0:128], re[:, 128:256], im[:, 0:128], im[:, 128:256])):
                    csend[h, gp * 8 : gp * 8 + 8, t * 4 + cb, :] = w

    def cchunk(h, d):
        return csend.at[h, pl.ds((d % 2) * 16 + ((d // 4) % 2) * 8 + ((d // 2) % 2) * 4 + (d // 8) * 2, 2)]

    def own_c(h):
        return pltpu.make_async_copy(cchunk(h, xy), crecv.at[h, :, xy], loc.at[9 + h])

    def send_c(h, k):
        m = (xy + k) % 16
        return remote(cchunk(h, m), crecv.at[h, :, xy], c_s.at[h, k], c_r.at[h, k], xydev(m))

    def start_c(h, g):
        @pl.when(xy % 2 == g)
        def _():
            own_c(h).start()

        first = (g + xy) % 2

        def one(i):
            k = 2 * i + first

            @pl.when(k > 0)
            def _():
                send_c(h, k).start()

        each(0, 8, one)

    def wait_c(h):
        own_c(h).wait()
        each(1, 16, lambda k: send_c(h, k).wait())

    own_q = drecv.at[n]

    def send_d(k):
        m = (z8 + k) % 8
        return remote(crecv.at[m % 2, (m % 4) // 2], own_q, d_s.at[k], d_r.at[k], z8dev(m))

    own_d = pltpu.make_async_copy(crecv.at[par, zlo // 2], own_q, loc.at[8])

    def send_e0():
        return remote(crecv.at[par, zlo // 2], own_q, e_s.at[0], e_r.at[0], sib)

    def send_e(k):
        m = (z8 + 8 - k) % 8
        q = ((m // 4) * 2 + core) * 4 + m % 4
        return remote(drecv.at[q], drecv.at[q], e_s.at[k], e_r.at[k], sib)

    def turn(k, side):
        m = (z8 + 8 - k) % 8
        q = ((m // 4) * 2 + side) * 4 + m % 4
        for s in range(8):
            o_ref[s // 4, q, :, (s % 4) * 128 : (s % 4) * 128 + 128] = drecv[q, :, s, :]

    def start_d(h):
        def one(k):
            @pl.when((z8 + k) % 2 == h)
            def _():
                send_d(k).start()

        each(1, 8, one)

        @pl.when(par == h)
        def _():
            own_d.start()
            send_e0().start()

    own_x.wait()
    each(1, 16, lambda k: send_a(0, k).wait())
    levels01(0)
    own_auxb.wait()
    each(1, 16, lambda k: send_aux_b(k).wait())
    each(0, 32, table2, 2)
    each(0, 8, table5, 2)
    each(1, 16, lambda k: send_a(1, k).wait())
    levels01(1)
    for g in range(2):
        wait_b(0, g)
        levels25(0, g)
        start_c(0, g)
    for g in range(2):
        wait_b(1, g)
        levels25(1, g)
        start_c(1, g)
        if g == 0:
            wait_c(0)
            start_d(0)
    wait_c(1)
    start_d(1)

    def forward(k):
        send_d(k).wait()
        send_e(k).start()
        turn(k, core)

    own_d.wait()
    turn(0, core)
    each(1, 8, forward)
    send_e0().wait()
    turn(0, 1 - core)

    def last(k):
        send_e(k).wait()
        turn(k, 1 - core)

    each(1, 8, last)


def body(coeffs, src_pos, tgt_pos, interp):
    x = coeffs.reshape(2, 16, 16, 512)
    vm = pltpu.VMEM
    dma = pltpu.SemaphoreType.DMA
    result = pl.pallas_call(
        kernel,
        out_shape=pltpu.VMEM((2, 16, 16, 512), F32),
        in_specs=[pl.BlockSpec(memory_space=pl.ANY)] * 4,
        out_specs=pl.BlockSpec(memory_space=pltpu.VMEM),
        scratch_shapes=[
            vm((2, 64), jnp.int32),
            vm((2, 32), jnp.int32),
            vm((8, 128), F32),
            vm((16, 8, 128), F32),
            vm((16, 2, 16, 128), F32),
            vm((2, 16, 128), F32),
            vm((2, 16, 16, 512), F32),
            vm((2, 512, 512), F32),
            vm((2, 2, 512, 256), BF16),
            vm((2, 2, 512, 256), BF16),
            vm((2, 16, 16, 256), BF16),
            vm((2, 16, 16, 256), BF16),
            vm((2, 16, 16, 256), F32),
            vm((5, 2, 16, 256), F32),
            vm((3, 32, 2, 16, 256), F32),
            vm((2, 2, 4, 2, 8, 256), F32),
            vm((2, 2, 512, 128), F32),
            vm((2, 2, 16, 32, 128), F32),
            vm((2, 32, 8, 128), F32),
            vm((2, 2, 16, 8, 128), F32),
            vm((16, 16, 8, 128), F32),
            dma((16,)), dma((16,)), dma((2, 16)), dma((2, 16)), dma((16,)), dma((16,)), dma((2, 2, 16)), dma((2, 2, 16)),
            dma((2, 16)), dma((2, 16)), dma((8,)), dma((8,)), dma((8,)), dma((8,)), dma((11,)),
        ],
        compiler_params=pltpu.CompilerParams(collective_id=0, has_side_effects=True),
    )(x, src_pos[0].T, tgt_pos.T, interp)
    return result.reshape(32, 16, 512)


def solution(mesh):
    in_specs = (P("angle", "box", None, None), P("angle", None, None), P("box", None), P())
    return jax.shard_map(body, mesh=mesh, in_specs=in_specs, out_specs=P("box", None, None), check_vma=False)
```

```python
import math

import jax
import jax.numpy as jnp
from jax import lax
from jax.experimental import pallas as pl
from jax.experimental.pallas import tpu as pltpu
from jax.sharding import PartitionSpec as P

MESH = pl.DeviceIdType.MESH
F32 = jnp.float32
BF16 = jnp.bfloat16
TWO_PI = 2.0 * math.pi


def cos_sin(turns):
    r = (turns - jnp.floor(turns + 0.5)) * math.pi
    x = r * r
    s = r * (2.0 + x * (-2.0 / 6 + x * (2.0 / 120 + x * (-2.0 / 5040 + x * (2.0 / 362880 + x * (-2.0 / 39916800))))))
    c = 1.0 + x * (
        -0.5 + x * (1.0 / 24 + x * (-1.0 / 720 + x * (1.0 / 40320 + x * (-1.0 / 3628800 + x * (1.0 / 479001600)))))
    )
    return 1.0 - 0.5 * (s * s), s * c


def split(value):
    hi = value.astype(BF16)
    lo = (value - hi.astype(F32)).astype(BF16)
    return hi, lo


def kernel(
    x_ref, src_ref, tgt_ref, w_ref, o_ref,
    srcv, tgtv, aux_o, aux_a, aux_b, auxf, ra, wf, whi, wlo, lhi, llo, out, tab1, tab2, tab5, bsend, brecv, csend, crecv, drecv,
    sa_s, sa_r, sx_s, sx_r, ba_s, ba_r, bx_s, bx_r, c_s, c_r, d_s, d_r, e_s, e_r, loc,
):
    box = lax.axis_index("box")
    ang = lax.axis_index("angle")
    xy = box // 4
    zlo = box % 4
    par = zlo % 2
    n = ang * 4 + zlo
    row = par * 8 + ang * 2 + zlo // 2
    core = ang % 2
    z8 = (ang // 2) * 4 + zlo

    def zdev(m):
        return {"box": xy * 4 + m % 4, "angle": m // 4}

    def xydev(m):
        return {"box": m * 4 + zlo, "angle": ang}

    def z8dev(m):
        return {"box": xy * 4 + m % 4, "angle": (m // 4) * 2 + core}

    sib = {"box": box, "angle": ang + 1 - 2 * core}

    def each(lo, hi, fn, un=1):
        def step(k, carry):
            for j in range(un):
                fn(lo + k * un + j)
            return carry

        lax.fori_loop(0, (hi - lo) // un, step, 0)

    def remote(src, dst, ss, rs, dev):
        return pltpu.make_async_remote_copy(src, dst, ss, rs, device_id=dev, device_id_type=MESH)

    barrier = pltpu.get_barrier_semaphore()
    each(1, 16, lambda k: pl.semaphore_signal(barrier, inc=1, device_id=zdev((n + k) % 16), device_id_type=MESH))
    each(1, 16, lambda k: pl.semaphore_signal(barrier, inc=1, device_id=xydev((xy + k) % 16), device_id_type=MESH))

    small = [pltpu.make_async_copy(src_ref, srcv, loc.at[2]), pltpu.make_async_copy(tgt_ref, tgtv, loc.at[3])]
    for copy in small:
        copy.start()
    wcopy = pltpu.make_async_copy(w_ref, wf, loc.at[0])
    wcopy.start()
    own_x = pltpu.make_async_copy(x_ref.at[:, n], ra.at[:, n], loc.at[1])
    own_x.start()
    for copy in small:
        copy.wait()
    lane2 = lax.broadcasted_iota(jnp.int32, (2, 128), 1)
    info = jnp.concatenate([tgtv[...].astype(F32), jnp.zeros((2, 96), F32)], axis=1)
    srcs = jnp.concatenate([srcv[...].astype(F32), jnp.zeros((2, 64), F32)], axis=1)
    for b in range(6):
        first = box // 2**b * 2**b
        total = jnp.sum(jnp.where((lane2 >= first) & (lane2 < first + 2**b), srcs, 0.0), axis=1, keepdims=True)
        info = jnp.where(lane2 == 32 + b, total, info)
    aux_o[...] = info
    own_aux = pltpu.make_async_copy(aux_o, aux_a.at[row], loc.at[2])
    own_aux.start()
    pl.semaphore_wait(barrier, 30)

    def send_aux_a(k):
        return remote(aux_o, aux_a.at[row], sa_s.at[k], sa_r.at[k], zdev((n + k) % 16))

    def send_a(h, k):
        m = (n + k) % 16
        return remote(x_ref.at[h, m], ra.at[h, n], sx_s.at[h, k], sx_r.at[h, k], zdev(m))

    each(1, 16, lambda k: send_aux_a(k).start())
    for h in range(2):
        each(1, 16, lambda k: send_a(h, k).start())

    wcopy.wait()
    for level in range(2):
        for t in range(2):
            hi, lo = split(wf[level, :, t * 256 : (t + 1) * 256])
            whi[level, t] = hi
            wlo[level, t] = lo

    own_aux.wait()
    each(1, 16, lambda k: send_aux_a(k).wait())
    for i in range(2):
        auxf[i] = jnp.concatenate([aux_a[r, i : i + 1, :] for r in range(16)], axis=0)
    own_auxb = pltpu.make_async_copy(auxf, aux_b.at[xy], loc.at[3])
    own_auxb.start()

    def send_aux_b(k):
        return remote(auxf, aux_b.at[xy], ba_s.at[k], ba_r.at[k], xydev((xy + k) % 16))

    each(1, 16, lambda k: send_aux_b(k).start())

    point = lax.broadcasted_iota(jnp.int32, (8, 256), 1)
    node_u, _ = cos_sin((2.0 * (point // 16).astype(F32) + 1.0) / 64.0)
    node_v, _ = cos_sin((2.0 * (point % 16).astype(F32) + 1.0) / 64.0)

    def tgt(ax, ay, t):
        hit = lax.broadcasted_iota(jnp.int32, ax.shape, 1) == t * 16 + n
        return [jnp.sum(jnp.where(hit, a, 0.0), axis=1, keepdims=True) for a in (ax, ay)]

    def src(ax, ay, b):
        return ax[:, 32 + b : 33 + b], ay[:, 32 + b : 33 + b]

    def phases(cu, cv):
        rows = cu.shape[0]
        cu = jnp.broadcast_to(cu, (rows, 256))
        cv = jnp.broadcast_to(cv, (rows, 256))
        u = jnp.concatenate([node_u] * (rows // 8), axis=0)
        v = jnp.concatenate([node_v] * (rows // 8), axis=0)
        return cos_sin(cu * u + cv * v)

    def ts(level):
        return 1.0 / (32.0 * (level + 1.0))

    def cs(level):
        return -1.0 / (32.0 * 2.0**level)

    ax, ay = auxf[0], auxf[1]
    s0 = src(ax, ay, 0)
    tab1[0, 0], tab1[0, 1] = phases(s0[0] * cs(0), s0[1] * cs(0))
    for t in range(2):
        tx, ty = tgt(ax, ay, t)
        for level in range(2):
            cx, cy = src(ax, ay, level + 1)
            c, s = phases(tx * ts(level) + cx * cs(level + 1), ty * ts(level) + cy * cs(level + 1))
            tab1[1 + 2 * level + t, 0], tab1[1 + 2 * level + t, 1] = c, s

    def table2(i):
        d, t = i // 2, i % 2
        ax, ay = aux_b[d, 0], aux_b[d, 1]
        tx, ty = tgt(ax, ay, t)
        for level in (2, 3, 4):
            cx, cy = src(ax, ay, level + 1)
            c, s = phases(tx * ts(level) + cx * cs(level + 1), ty * ts(level) + cy * cs(level + 1))
            tab2[level - 2, i, 0], tab2[level - 2, i, 1] = c, s

    srow = lax.broadcasted_iota(jnp.int32, (8, 128), 0)
    srow2 = lax.broadcasted_iota(jnp.int32, (8, 256), 0)

    def pick(rows, values):
        a, b, c, d = values
        return jnp.where(rows < 4, jnp.where(rows < 2, a, b), jnp.where(rows < 6, c, d))

    def table5(i):
        pp, h = i // 2, i % 2
        ax, ay = [
            pick(
                srow,
                [aux_b[4 * (pp % 2) + 2 * p2 + 8 * h5 + pp // 2, e, pl.ds(pl.multiple_of(h * 8, 8), 8), :] for p2 in range(2) for h5 in range(2)],
            )
            for e in range(2)
        ]
        for t in range(2):
            tx, ty = tgt(ax, ay, t)
            tab5[h, t, pp, 0], tab5[h, t, pp, 1] = phases(tx * ts(5), ty * ts(5))

    def rotated(re, im, c, s):
        return re * c - im * s, re * s + im * c

    def place(d, t, bit):
        stride = 1 << bit
        c = (d // stride) % 2
        return d - c * stride + t * stride, c

    def matmul(level, blocks, sides=(0, 1)):
        w = level % 2
        rows = blocks * 16
        for t in sides:
            high = [lhi[c, 0:blocks].reshape(rows, 256) for c in range(2)]
            low = [llo[c, 0:blocks].reshape(rows, 256) for c in range(2)]
            left = jnp.concatenate([*high, *low, *high], axis=1)
            right = jnp.concatenate([whi[w, t], whi[w, t], wlo[w, t]], axis=0)
            acc = jnp.dot(left, right, preferred_element_type=F32)
            out[t, 0:blocks] = acc.reshape(blocks, 16, 256)

    def put(c, block, value):
        lhi[c, block], llo[c, block] = split(value)

    def levels01(h):
        def build0(i):
            j, b0 = i // 2, i % 2
            v = ra[h, (j // 2) * 4 + (j % 2) * 2 + b0]
            r = pl.ds(b0 * 8 + j, 1)
            re, im = rotated(v[:, 0:256], v[:, 256:512], tab1[0, 0, r, :], tab1[0, 1, r, :])
            put(b0, 2 * j, re)
            put(b0, 2 * j + 1, im)

        each(0, 16, build0, 4)
        matmul(0, 16)

        def build1(i):
            j, t = i // 2, i % 2
            r = pl.ds(h * 8 + j, 1)
            re, im = rotated(out[t, 2 * j], out[t, 2 * j + 1], tab1[1 + t, 0, r, :], tab1[1 + t, 1, r, :])
            b, c = place(j, t, 0)
            put(c, 2 * b, re)
            put(c, 2 * b + 1, im)

        each(0, 16, build1, 4)
        for t in range(2):
            matmul(1, 16, (t,))

            def post1(j):
                r = pl.ds(h * 8 + j, 1)
                re, im = rotated(out[t, 2 * j], out[t, 2 * j + 1], tab1[3 + t, 0, r, :], tab1[3 + t, 1, r, :])
                for cb, v in enumerate((re[:, 0:128], re[:, 128:256], im[:, 0:128], im[:, 128:256])):
                    bsend[h, t, pl.ds(cb * 8 + j, 16, stride=32), :] = v

            each(0, 8, post1, 4)
            start_b(h, t)

    def bchunk(h, t, f):
        return bsend.at[h, t, pl.ds(pl.multiple_of(f * 32, 32), 32), :]

    def own_b(h, t):
        return pltpu.make_async_copy(bchunk(h, t, xy), brecv.at[h, t, xy], loc.at[4 + 2 * h + t])

    def send_b(h, t, k):
        m = (xy + k) % 16
        return remote(bchunk(h, t, m), brecv.at[h, t, xy], bx_s.at[h, t, k], bx_r.at[h, t, k], xydev(m))

    def start_b(h, t):
        own_b(h, t).start()
        each(1, 16, lambda k: send_b(h, t, k).start())

    def wait_b(h, t):
        own_b(h, t).wait()
        each(1, 16, lambda k: send_b(h, t, k).wait())

    def levels25(h, g):
        half = slice(h * 8, h * 8 + 8)

        def build2(d):
            v = [brecv[h, g, d, cb * 8 : cb * 8 + 8, :] for cb in range(4)]
            put(d % 2, d // 2, jnp.concatenate([jnp.concatenate(v[0:2], axis=1), jnp.concatenate(v[2:4], axis=1)], axis=0))

        each(0, 16, build2, 4)
        matmul(2, 8)
        for bit in (0, 1):

            def build34(i):
                j, t = i // 2, i % 2
                v = out[t, j]
                r = 4 * j + 2 * g + t
                re, im = rotated(v[0:8], v[8:16], tab2[bit, r, 0, half, :], tab2[bit, r, 1, half, :])
                b, c = place(j, t, bit)
                put(c, b, jnp.concatenate([re, im], axis=0))

            each(0, 16, build34, 4)
            matmul(bit + 3, 8)

        def build5(i):
            pp, c = i // 2, i % 2
            sums = [[], []]
            for p2 in range(2):
                for t in range(2):
                    j = 2 * pp + p2 + 4 * c
                    v = out[t, j]
                    r = 4 * j + 2 * g + t
                    both = rotated(v[0:8], v[8:16], tab2[2, r, 0, half, :], tab2[2, r, 1, half, :])
                    for e in range(2):
                        w = both[e] + pltpu.roll(both[e], 4, 0)
                        sums[e].append(w + pltpu.roll(w, 2, 0))
            put(c, pp, jnp.concatenate([pick(srow2, sums[0]), pick(srow2, sums[1])], axis=0))

        each(0, 4, build5, 4)
        matmul(5, 2)

        for pp in range(2):
            gp = g * 2 + pp
            for t in range(2):
                v = out[t, pp]
                re, im = rotated(v[0:8], v[8:16], tab5[h, t, gp, 0], tab5[h, t, gp, 1])
                for cb, w in enumerate((re[:, 0:128], re[:, 128:256], im[:, 0:128], im[:, 128:256])):
                    csend[h, gp * 8 : gp * 8 + 8, t * 4 + cb, :] = w

    def cchunk(h, d):
        return csend.at[h, pl.ds((d % 2) * 16 + ((d // 4) % 2) * 8 + ((d // 2) % 2) * 4 + (d // 8) * 2, 2)]

    def own_c(h):
        return pltpu.make_async_copy(cchunk(h, xy), crecv.at[h, :, xy], loc.at[9 + h])

    def send_c(h, k):
        m = (xy + k) % 16
        return remote(cchunk(h, m), crecv.at[h, :, xy], c_s.at[h, k], c_r.at[h, k], xydev(m))

    def start_c(h, g):
        @pl.when(xy % 2 == g)
        def _():
            own_c(h).start()

        first = (g + xy) % 2

        def one(i):
            k = 2 * i + first

            @pl.when(k > 0)
            def _():
                send_c(h, k).start()

        each(0, 8, one)

    def wait_c(h):
        own_c(h).wait()
        each(1, 16, lambda k: send_c(h, k).wait())

    own_q = drecv.at[n]

    def send_d(k):
        m = (z8 + k) % 8
        return remote(crecv.at[m % 2, (m % 4) // 2], own_q, d_s.at[k], d_r.at[k], z8dev(m))

    own_d = pltpu.make_async_copy(crecv.at[par, zlo // 2], own_q, loc.at[8])

    def send_e0():
        return remote(crecv.at[par, zlo // 2], own_q, e_s.at[0], e_r.at[0], sib)

    def send_e(k):
        m = (z8 + 8 - k) % 8
        q = ((m // 4) * 2 + core) * 4 + m % 4
        return remote(drecv.at[q], drecv.at[q], e_s.at[k], e_r.at[k], sib)

    def turn(k, side):
        m = (z8 + 8 - k) % 8
        q = ((m // 4) * 2 + side) * 4 + m % 4
        for s in range(8):
            o_ref[s // 4, q, :, (s % 4) * 128 : (s % 4) * 128 + 128] = drecv[q, :, s, :]

    def start_d(h):
        def one(k):
            @pl.when((z8 + k) % 2 == h)
            def _():
                send_d(k).start()

        each(1, 8, one)

        @pl.when(par == h)
        def _():
            own_d.start()
            send_e0().start()

    own_x.wait()
    each(1, 16, lambda k: send_a(0, k).wait())
    levels01(0)
    own_auxb.wait()
    each(1, 16, lambda k: send_aux_b(k).wait())
    each(0, 32, table2, 2)
    each(0, 8, table5, 2)
    each(1, 16, lambda k: send_a(1, k).wait())
    levels01(1)
    for g in range(2):
        wait_b(0, g)
        levels25(0, g)
        start_c(0, g)
    for g in range(2):
        wait_b(1, g)
        levels25(1, g)
        start_c(1, g)
        if g == 0:
            wait_c(0)
            start_d(0)
    wait_c(1)
    start_d(1)

    def forward(k):
        send_d(k).wait()
        send_e(k).start()
        turn(k, core)

    own_d.wait()
    turn(0, core)
    each(1, 8, forward)
    send_e0().wait()
    turn(0, 1 - core)

    def last(k):
        send_e(k).wait()
        turn(k, 1 - core)

    each(1, 8, last)


def body(coeffs, src_pos, tgt_pos, interp):
    x = coeffs.reshape(2, 16, 16, 512)
    vm = pltpu.VMEM
    dma = pltpu.SemaphoreType.DMA
    result = pl.pallas_call(
        kernel,
        out_shape=pltpu.VMEM((2, 16, 16, 512), F32),
        in_specs=[pl.BlockSpec(memory_space=pl.ANY)] * 4,
        out_specs=pl.BlockSpec(memory_space=pltpu.VMEM),
        scratch_shapes=[
            vm((2, 64), jnp.int32),
            vm((2, 32), jnp.int32),
            vm((2, 128), F32),
            vm((16, 2, 128), F32),
            vm((16, 2, 16, 128), F32),
            vm((2, 16, 128), F32),
            vm((2, 16, 16, 512), F32),
            vm((2, 512, 512), F32),
            vm((2, 2, 512, 256), BF16),
            vm((2, 2, 512, 256), BF16),
            vm((2, 16, 16, 256), BF16),
            vm((2, 16, 16, 256), BF16),
            vm((2, 16, 16, 256), F32),
            vm((5, 2, 16, 256), F32),
            vm((3, 32, 2, 16, 256), F32),
            vm((2, 2, 4, 2, 8, 256), F32),
            vm((2, 2, 512, 128), F32),
            vm((2, 2, 16, 32, 128), F32),
            vm((2, 32, 8, 128), F32),
            vm((2, 2, 16, 8, 128), F32),
            vm((16, 16, 8, 128), F32),
            dma((16,)), dma((16,)), dma((2, 16)), dma((2, 16)), dma((16,)), dma((16,)), dma((2, 2, 16)), dma((2, 2, 16)),
            dma((2, 16)), dma((2, 16)), dma((8,)), dma((8,)), dma((8,)), dma((8,)), dma((11,)),
        ],
        compiler_params=pltpu.CompilerParams(collective_id=0, has_side_effects=True),
    )(x, src_pos[0].T, tgt_pos.T, interp)
    return result.reshape(32, 16, 512)


def solution(mesh):
    in_specs = (P("angle", "box", None, None), P("angle", None, None), P("box", None), P())
    return jax.shard_map(body, mesh=mesh, in_specs=in_specs, out_specs=P("box", None, None), check_vma=False)
```

```python
import math

import jax
import jax.numpy as jnp
from jax import lax
from jax.experimental import pallas as pl
from jax.experimental.pallas import tpu as pltpu
from jax.sharding import PartitionSpec as P

MESH = pl.DeviceIdType.MESH
F32 = jnp.float32
BF16 = jnp.bfloat16
TWO_PI = 2.0 * math.pi


def cos_sin(turns):
    r = (turns - jnp.floor(turns + 0.5)) * math.pi
    x = r * r
    s = r * (2.0 + x * (-2.0 / 6 + x * (2.0 / 120 + x * (-2.0 / 5040 + x * (2.0 / 362880 + x * (-2.0 / 39916800))))))
    c = 1.0 + x * (
        -0.5 + x * (1.0 / 24 + x * (-1.0 / 720 + x * (1.0 / 40320 + x * (-1.0 / 3628800 + x * (1.0 / 479001600)))))
    )
    return 1.0 - 0.5 * (s * s), s * c


def split(value):
    hi = value.astype(BF16)
    lo = (value - hi.astype(F32)).astype(BF16)
    return hi, lo


def kernel(
    x_ref, src_ref, tgt_ref, w_ref, o_ref,
    srcv, tgtv, aux_o, aux_a, aux_b, auxf, ra, wf, whi, wlo, lhi, llo, out, tab1, tab2, tab5, bsend, brecv, csend, crecv, drecv,
    sa_s, sa_r, sx_s, sx_r, ba_s, ba_r, bx_s, bx_r, c_s, c_r, d_s, d_r, e_s, e_r, loc,
):
    box = lax.axis_index("box")
    ang = lax.axis_index("angle")
    xy = box // 4
    zlo = box % 4
    par = zlo % 2
    n = ang * 4 + zlo
    row = par * 8 + ang * 2 + zlo // 2
    core = ang % 2
    z8 = (ang // 2) * 4 + zlo

    def zdev(m):
        return {"box": xy * 4 + m % 4, "angle": m // 4}

    def xydev(m):
        return {"box": m * 4 + zlo, "angle": ang}

    def z8dev(m):
        return {"box": xy * 4 + m % 4, "angle": (m // 4) * 2 + core}

    sib = {"box": box, "angle": ang + 1 - 2 * core}

    def each(lo, hi, fn, un=1):
        def step(k, carry):
            for j in range(un):
                fn(lo + k * un + j)
            return carry

        lax.fori_loop(0, (hi - lo) // un, step, 0)

    def remote(src, dst, ss, rs, dev):
        return pltpu.make_async_remote_copy(src, dst, ss, rs, device_id=dev, device_id_type=MESH)

    barrier = pltpu.get_barrier_semaphore()
    each(1, 16, lambda k: pl.semaphore_signal(barrier, inc=1, device_id=zdev((n + k) % 16), device_id_type=MESH))
    each(1, 16, lambda k: pl.semaphore_signal(barrier, inc=1, device_id=xydev((xy + k) % 16), device_id_type=MESH))

    small = [pltpu.make_async_copy(src_ref, srcv, loc.at[2]), pltpu.make_async_copy(tgt_ref, tgtv, loc.at[3])]
    for copy in small:
        copy.start()
    wcopy = pltpu.make_async_copy(w_ref, wf, loc.at[0])
    wcopy.start()
    own_x = pltpu.make_async_copy(x_ref.at[:, n], ra.at[:, n], loc.at[1])
    own_x.start()
    for copy in small:
        copy.wait()
    lane2 = lax.broadcasted_iota(jnp.int32, (2, 128), 1)
    info = jnp.concatenate([tgtv[...].astype(F32), jnp.zeros((2, 96), F32)], axis=1)
    srcs = jnp.concatenate([srcv[...].astype(F32), jnp.zeros((2, 64), F32)], axis=1)
    for b in range(6):
        first = box // 2**b * 2**b
        total = jnp.sum(jnp.where((lane2 >= first) & (lane2 < first + 2**b), srcs, 0.0), axis=1, keepdims=True)
        info = jnp.where(lane2 == 32 + b, total, info)
    aux_o[...] = info
    own_aux = pltpu.make_async_copy(aux_o, aux_a.at[row], loc.at[2])
    own_aux.start()
    pl.semaphore_wait(barrier, 30)

    def send_aux_a(k):
        return remote(aux_o, aux_a.at[row], sa_s.at[k], sa_r.at[k], zdev((n + k) % 16))

    def send_a(h, k):
        m = (n + k) % 16
        return remote(x_ref.at[h, m], ra.at[h, n], sx_s.at[h, k], sx_r.at[h, k], zdev(m))

    each(1, 16, lambda k: send_aux_a(k).start())
    for h in range(2):
        each(1, 16, lambda k: send_a(h, k).start())

    wcopy.wait()
    for level in range(2):
        for t in range(2):
            hi, lo = split(wf[level, :, t * 256 : (t + 1) * 256])
            whi[level, t] = hi
            wlo[level, t] = lo

    own_aux.wait()
    each(1, 16, lambda k: send_aux_a(k).wait_recv())
    for i in range(2):
        auxf[i] = jnp.concatenate([aux_a[r, i : i + 1, :] for r in range(16)], axis=0)
    own_auxb = pltpu.make_async_copy(auxf, aux_b.at[xy], loc.at[3])
    own_auxb.start()

    def send_aux_b(k):
        return remote(auxf, aux_b.at[xy], ba_s.at[k], ba_r.at[k], xydev((xy + k) % 16))

    each(1, 16, lambda k: send_aux_b(k).start())

    point = lax.broadcasted_iota(jnp.int32, (8, 256), 1)
    node_u, _ = cos_sin((2.0 * (point // 16).astype(F32) + 1.0) / 64.0)
    node_v, _ = cos_sin((2.0 * (point % 16).astype(F32) + 1.0) / 64.0)

    def tgt(ax, ay, t):
        hit = lax.broadcasted_iota(jnp.int32, ax.shape, 1) == t * 16 + n
        return [jnp.sum(jnp.where(hit, a, 0.0), axis=1, keepdims=True) for a in (ax, ay)]

    def src(ax, ay, b):
        return ax[:, 32 + b : 33 + b], ay[:, 32 + b : 33 + b]

    def phases(cu, cv):
        rows = cu.shape[0]
        cu = jnp.broadcast_to(cu, (rows, 256))
        cv = jnp.broadcast_to(cv, (rows, 256))
        u = jnp.concatenate([node_u] * (rows // 8), axis=0)
        v = jnp.concatenate([node_v] * (rows // 8), axis=0)
        return cos_sin(cu * u + cv * v)

    def ts(level):
        return 1.0 / (32.0 * (level + 1.0))

    def cs(level):
        return -1.0 / (32.0 * 2.0**level)

    ax, ay = auxf[0], auxf[1]
    s0 = src(ax, ay, 0)
    tab1[0, 0], tab1[0, 1] = phases(s0[0] * cs(0), s0[1] * cs(0))
    for t in range(2):
        tx, ty = tgt(ax, ay, t)
        for level in range(2):
            cx, cy = src(ax, ay, level + 1)
            c, s = phases(tx * ts(level) + cx * cs(level + 1), ty * ts(level) + cy * cs(level + 1))
            tab1[1 + 2 * level + t, 0], tab1[1 + 2 * level + t, 1] = c, s

    def table2(i):
        d, t = i // 2, i % 2
        ax, ay = aux_b[d, 0], aux_b[d, 1]
        tx, ty = tgt(ax, ay, t)
        for level in (2, 3, 4):
            cx, cy = src(ax, ay, level + 1)
            c, s = phases(tx * ts(level) + cx * cs(level + 1), ty * ts(level) + cy * cs(level + 1))
            tab2[level - 2, i, 0], tab2[level - 2, i, 1] = c, s

    srow = lax.broadcasted_iota(jnp.int32, (8, 128), 0)
    srow2 = lax.broadcasted_iota(jnp.int32, (8, 256), 0)

    def pick(rows, values):
        a, b, c, d = values
        return jnp.where(rows < 4, jnp.where(rows < 2, a, b), jnp.where(rows < 6, c, d))

    def table5(i):
        pp, h = i // 2, i % 2
        ax, ay = [
            pick(
                srow,
                [aux_b[4 * (pp % 2) + 2 * p2 + 8 * h5 + pp // 2, e, pl.ds(pl.multiple_of(h * 8, 8), 8), :] for p2 in range(2) for h5 in range(2)],
            )
            for e in range(2)
        ]
        for t in range(2):
            tx, ty = tgt(ax, ay, t)
            tab5[h, t, pp, 0], tab5[h, t, pp, 1] = phases(tx * ts(5), ty * ts(5))

    def rotated(re, im, c, s):
        return re * c - im * s, re * s + im * c

    def place(d, t, bit):
        stride = 1 << bit
        c = (d // stride) % 2
        return d - c * stride + t * stride, c

    def matmul(level, blocks, sides=(0, 1)):
        w = level % 2
        rows = blocks * 16
        for t in sides:
            high = [lhi[c, 0:blocks].reshape(rows, 256) for c in range(2)]
            low = [llo[c, 0:blocks].reshape(rows, 256) for c in range(2)]
            left = jnp.concatenate([*high, *low, *high], axis=1)
            right = jnp.concatenate([whi[w, t], whi[w, t], wlo[w, t]], axis=0)
            acc = jnp.dot(left, right, preferred_element_type=F32)
            out[t, 0:blocks] = acc.reshape(blocks, 16, 256)

    def put(c, block, value):
        lhi[c, block], llo[c, block] = split(value)

    def levels01(h):
        def build0(i):
            j, b0 = i // 2, i % 2
            v = ra[h, (j // 2) * 4 + (j % 2) * 2 + b0]
            r = pl.ds(b0 * 8 + j, 1)
            re, im = rotated(v[:, 0:256], v[:, 256:512], tab1[0, 0, r, :], tab1[0, 1, r, :])
            put(b0, 2 * j, re)
            put(b0, 2 * j + 1, im)

        each(0, 16, build0, 4)
        matmul(0, 16)

        def build1(i):
            j, t = i // 2, i % 2
            r = pl.ds(h * 8 + j, 1)
            re, im = rotated(out[t, 2 * j], out[t, 2 * j + 1], tab1[1 + t, 0, r, :], tab1[1 + t, 1, r, :])
            b, c = place(j, t, 0)
            put(c, 2 * b, re)
            put(c, 2 * b + 1, im)

        each(0, 16, build1, 4)
        for t in range(2):
            matmul(1, 16, (t,))

            def post1(j):
                r = pl.ds(h * 8 + j, 1)
                re, im = rotated(out[t, 2 * j], out[t, 2 * j + 1], tab1[3 + t, 0, r, :], tab1[3 + t, 1, r, :])
                for cb, v in enumerate((re[:, 0:128], re[:, 128:256], im[:, 0:128], im[:, 128:256])):
                    bsend[h, t, pl.ds(cb * 8 + j, 16, stride=32), :] = v

            each(0, 8, post1, 4)
            start_b(h, t)

    def bchunk(h, t, f):
        return bsend.at[h, t, pl.ds(pl.multiple_of(f * 32, 32), 32), :]

    def own_b(h, t):
        return pltpu.make_async_copy(bchunk(h, t, xy), brecv.at[h, t, xy], loc.at[4 + 2 * h + t])

    def send_b(h, t, k):
        m = (xy + k) % 16
        return remote(bchunk(h, t, m), brecv.at[h, t, xy], bx_s.at[h, t, k], bx_r.at[h, t, k], xydev(m))

    def start_b(h, t):
        own_b(h, t).start()
        each(1, 16, lambda k: send_b(h, t, k).start())

    def wait_b(h, t):
        own_b(h, t).wait()
        each(1, 16, lambda k: send_b(h, t, k).wait_recv())

    def levels25(h, g):
        half = slice(h * 8, h * 8 + 8)

        def build2(d):
            v = [brecv[h, g, d, cb * 8 : cb * 8 + 8, :] for cb in range(4)]
            put(d % 2, d // 2, jnp.concatenate([jnp.concatenate(v[0:2], axis=1), jnp.concatenate(v[2:4], axis=1)], axis=0))

        each(0, 16, build2, 4)
        matmul(2, 8)
        for bit in (0, 1):

            def build34(i):
                j, t = i // 2, i % 2
                v = out[t, j]
                r = 4 * j + 2 * g + t
                re, im = rotated(v[0:8], v[8:16], tab2[bit, r, 0, half, :], tab2[bit, r, 1, half, :])
                b, c = place(j, t, bit)
                put(c, b, jnp.concatenate([re, im], axis=0))

            each(0, 16, build34, 4)
            matmul(bit + 3, 8)

        def build5(i):
            pp, c = i // 2, i % 2
            sums = [[], []]
            for p2 in range(2):
                for t in range(2):
                    j = 2 * pp + p2 + 4 * c
                    v = out[t, j]
                    r = 4 * j + 2 * g + t
                    both = rotated(v[0:8], v[8:16], tab2[2, r, 0, half, :], tab2[2, r, 1, half, :])
                    for e in range(2):
                        w = both[e] + pltpu.roll(both[e], 4, 0)
                        sums[e].append(w + pltpu.roll(w, 2, 0))
            put(c, pp, jnp.concatenate([pick(srow2, sums[0]), pick(srow2, sums[1])], axis=0))

        each(0, 4, build5, 4)
        matmul(5, 2)

        for pp in range(2):
            gp = g * 2 + pp
            for t in range(2):
                v = out[t, pp]
                re, im = rotated(v[0:8], v[8:16], tab5[h, t, gp, 0], tab5[h, t, gp, 1])
                for cb, w in enumerate((re[:, 0:128], re[:, 128:256], im[:, 0:128], im[:, 128:256])):
                    csend[h, gp * 8 : gp * 8 + 8, t * 4 + cb, :] = w

    def cchunk(h, d):
        return csend.at[h, pl.ds((d % 2) * 16 + ((d // 4) % 2) * 8 + ((d // 2) % 2) * 4 + (d // 8) * 2, 2)]

    def own_c(h):
        return pltpu.make_async_copy(cchunk(h, xy), crecv.at[h, :, xy], loc.at[9 + h])

    def send_c(h, k):
        m = (xy + k) % 16
        return remote(cchunk(h, m), crecv.at[h, :, xy], c_s.at[h, k], c_r.at[h, k], xydev(m))

    def start_c(h, g):
        @pl.when(xy % 2 == g)
        def _():
            own_c(h).start()

        first = (g + xy) % 2

        def one(i):
            k = 2 * i + first

            @pl.when(k > 0)
            def _():
                send_c(h, k).start()

        each(0, 8, one)

    own_q = drecv.at[n]

    def column(step):
        return (xy // 4 + (0, 1, 3, 2)[step]) % 4

    def send_d(step, k):
        m = (z8 + k) % 8
        fields = pl.ds(column(step) * 4, 4)
        return remote(
            crecv.at[m % 2, (m % 4) // 2, fields], drecv.at[n, fields], d_s.at[step, k], d_r.at[step, k], z8dev(m)
        )

    own_d = pltpu.make_async_copy(crecv.at[par, zlo // 2], own_q, loc.at[8])

    def send_e0():
        return remote(crecv.at[par, zlo // 2], own_q, e_s.at[0], e_r.at[0], sib)

    def send_e(k):
        m = (z8 + 8 - k) % 8
        q = ((m // 4) * 2 + core) * 4 + m % 4
        return remote(drecv.at[q], drecv.at[q], e_s.at[k], e_r.at[k], sib)

    def turn(k, side):
        m = (z8 + 8 - k) % 8
        q = ((m // 4) * 2 + side) * 4 + m % 4
        for s in range(8):
            o_ref[s // 4, q, :, (s % 4) * 128 : (s % 4) * 128 + 128] = drecv[q, :, s, :]

    def relay(h):
        for step in range(4):

            def arrived(y):
                k = (xy + 16 - column(step) * 4 - y) % 16

                @pl.when(k == 0)
                def _():
                    own_c(h).wait()

                @pl.when(k > 0)
                def _():
                    send_c(h, k).wait_recv()

            each(0, 4, arrived)

            def one(k):
                @pl.when((z8 + k) % 2 == h)
                def _():
                    send_d(step, k).start()

            each(1, 8, one)

        @pl.when(par == h)
        def _():
            own_d.start()
            send_e0().start()


    own_x.wait()
    each(1, 16, lambda k: send_a(0, k).wait_recv())
    levels01(0)
    own_auxb.wait()
    each(1, 16, lambda k: send_aux_b(k).wait_recv())
    each(0, 32, table2, 2)
    each(0, 8, table5, 2)
    each(1, 16, lambda k: send_a(1, k).wait_recv())
    levels01(1)
    for g in range(2):
        wait_b(0, g)
        levels25(0, g)
        start_c(0, g)
    for g in range(2):
        wait_b(1, g)
        levels25(1, g)
        start_c(1, g)
        if g == 0:
            relay(0)
    relay(1)

    def forward(k):
        for step in range(4):
            send_d(step, k).wait()
        send_e(k).start()
        turn(k, core)

    own_d.wait()
    turn(0, core)
    each(1, 8, forward)
    send_e0().wait()
    turn(0, 1 - core)

    def last(k):
        send_e(k).wait()
        turn(k, 1 - core)

    each(1, 8, last)

    def sent(k):
        send_aux_a(k).wait_send()
        send_aux_b(k).wait_send()
        for h in range(2):
            send_a(h, k).wait_send()
            send_c(h, k).wait_send()
            for t in range(2):
                send_b(h, t, k).wait_send()

    each(1, 16, sent)


def body(coeffs, src_pos, tgt_pos, interp):
    x = coeffs.reshape(2, 16, 16, 512)
    vm = pltpu.VMEM
    dma = pltpu.SemaphoreType.DMA
    result = pl.pallas_call(
        kernel,
        out_shape=pltpu.VMEM((2, 16, 16, 512), F32),
        in_specs=[pl.BlockSpec(memory_space=pl.ANY)] * 4,
        out_specs=pl.BlockSpec(memory_space=pltpu.VMEM),
        scratch_shapes=[
            vm((2, 64), jnp.int32),
            vm((2, 32), jnp.int32),
            vm((2, 128), F32),
            vm((16, 2, 128), F32),
            vm((16, 2, 16, 128), F32),
            vm((2, 16, 128), F32),
            vm((2, 16, 16, 512), F32),
            vm((2, 512, 512), F32),
            vm((2, 2, 512, 256), BF16),
            vm((2, 2, 512, 256), BF16),
            vm((2, 16, 16, 256), BF16),
            vm((2, 16, 16, 256), BF16),
            vm((2, 16, 16, 256), F32),
            vm((5, 2, 16, 256), F32),
            vm((3, 32, 2, 16, 256), F32),
            vm((2, 2, 4, 2, 8, 256), F32),
            vm((2, 2, 512, 128), F32),
            vm((2, 2, 16, 32, 128), F32),
            vm((2, 32, 8, 128), F32),
            vm((2, 2, 16, 8, 128), F32),
            vm((16, 16, 8, 128), F32),
            dma((16,)), dma((16,)), dma((2, 16)), dma((2, 16)), dma((16,)), dma((16,)), dma((2, 2, 16)), dma((2, 2, 16)),
            dma((2, 16)), dma((2, 16)), dma((4, 8)), dma((4, 8)), dma((8,)), dma((8,)), dma((11,)),
        ],
        compiler_params=pltpu.CompilerParams(collective_id=0, has_side_effects=True),
    )(x, src_pos[0].T, tgt_pos.T, interp)
    return result.reshape(32, 16, 512)


def solution(mesh):
    in_specs = (P("angle", "box", None, None), P("angle", None, None), P("box", None), P())
    return jax.shard_map(body, mesh=mesh, in_specs=in_specs, out_specs=P("box", None, None), check_vma=False)
```
